32 devices in a mesh: groups: 2 (over x), req: 4 (over y, core), fsdp: 4 (over z).
Axes of the slice: x: 2, y: 2, z: 4, core: 2. Of those that a mesh axis runs over, the one named last changes fastest.
Arguments:
- tokens: bfloat16 [2, 128, 8, 2048], P(None, ('groups', 'req', 'fsdp')), parts along dimension 1, may hold values from -6 to 6
- in_weight: bfloat16 [2048, 4224], P(('req', 'fsdp')), may hold values from -0.125 to 0.125
- dt_weight: bfloat16 [2048, 64], P(('req', 'fsdp')), may hold values from -0.125 to 0.125
- conv_weight: float32 [4, 4224], replicated, may hold values from -3 to 3
- conv_bias: float32 [4224], replicated, may hold values from -3 to 3
- dt_bias: float32 [64], replicated, may hold values from -2 to 1
- decay_rate: float32 [64], replicated, may hold values from 0.004 to 0.3
- skip_gain: float32 [64], replicated, may hold values from 0.5 to 1.5
- norm_gain: float32 [4096], replicated, may hold values from 0.5 to 1.5
- state_cache: bfloat16 [256, 64, 4096], P(('groups', 'req', 'fsdp')), parts along dimension 0, may hold values from -6 to 6
- conv_cache: bfloat16 [256, 3, 4224], P(('groups', 'req', 'fsdp')), parts along dimension 0, may hold values from -6 to 6
- hash_owner: int32 [128], P(('groups', 'req', 'fsdp')), parts along dimension 0, may hold values from 0 to 3, as said below
- cache_slot: int32 [128], P(('groups', 'req', 'fsdp')), parts along dimension 0, may hold values from 0 to 7, as said below
- event_counts: int32 [2, 128], P(None, ('groups', 'req', 'fsdp')), parts along dimension 1, may hold values from 1 to 8
Outputs:
- user_vectors: bfloat16 [2, 128, 4096], P(None, ('groups', 'req', 'fsdp')), parts along dimension 1
- new_states: bfloat16 [256, 64, 4096], P(('groups', 'req', 'fsdp')), parts along dimension 0
- new_windows: bfloat16 [256, 3, 4224], P(('groups', 'req', 'fsdp')), parts along dimension 0
The draws below stay inside these ranges and needn't reach their ends.
There are 2 independent parts, one for each index of `groups`. The reference program is written for one: setup_inputs(seed, part) draws one part's arguments, and reference() takes and returns one part's arrays. A program takes and returns all parts, laid end to end along the dimension named above; an argument that names none is the same for every part. Nothing has to cross between parts.
Inputs may be any that keep to these rules, and one draw needn't show every extreme that they name: `hash_owner`: among the users of one device at most 2 have the same owner, and some device has exactly 2 users of one owner. Among the users of all devices with one fsdp index at most 8 have the same owner, and some owner has exactly 8. `cache_slot`: users of one fsdp index with the same owner have distinct rows.
All inputs are finite; a program needn't handle non-finite values.
Results may differ from the reference program's by a relative error of at most 0.006.
Values may be sent and summed in bfloat16 or wider, within the bound.
A program may use at most 192 MiB of HBM per device.

```python
import math
import jax
import jax.numpy as jnp
from jax import lax

D = 2048
HEADS = 64
HEAD_DIM = 64
STATE = 64
KCONV = 4
STEPS = 2
USERS_DEV = 4
EV = 8
INNER = 4096
CONV_CH = 4224
CACHE = 8
USERS = 64
SLOTS = 128
N_REQ = 4
N_FSDP = 4


def owner_table(key):
    owners = N_REQ
    columns = N_FSDP
    per_device = USERS_DEV
    base_key = jax.random.fold_in(key, 7)
    key_perm, key_shift, key_order, key_slot = jax.random.split(base_key, 4)
    base_hot = 2 * per_device // owners
    extra_hot = 2 * per_device % owners
    req_index = jnp.arange(owners, dtype=jnp.int32)
    hot_count = base_hot + (req_index < extra_hot).astype(jnp.int32)
    position = jnp.arange(per_device, dtype=jnp.int32)
    shift = jax.random.randint(key_shift, (columns,), 0, max(owners - 1, 1)).astype(jnp.int32)
    remainder = position[None, None, :] - hot_count[:, None, None]
    label_rest = 1 + (req_index[:, None, None] + shift[None, :, None] + jnp.maximum(remainder, 0) // 2) % (owners - 1)
    label = jnp.where(remainder < 0, 0, label_rest)
    relabel = jax.vmap(lambda one_key: jax.random.permutation(one_key, owners))(jax.random.split(key_perm, columns)).astype(jnp.int32)
    column_index = jnp.arange(columns, dtype=jnp.int32)
    owner_grid = relabel[column_index[None, :, None], label]
    order = jax.vmap(lambda one_key: jax.random.permutation(one_key, per_device))(jax.random.split(key_order, owners * columns)).astype(jnp.int32)
    order = order.reshape(owners, columns, per_device)
    owner_grid = jnp.take_along_axis(owner_grid, order, axis=2)
    column_major = owner_grid.transpose(1, 0, 2).reshape(columns, owners * per_device)
    matches = (column_major[:, :, None] == jnp.arange(owners, dtype=jnp.int32)[None, None, :]).astype(jnp.int32)
    earlier = jnp.cumsum(matches, axis=1) - matches
    ranking = jnp.sum(earlier * matches, axis=2)
    slot_perm = jax.vmap(lambda one_key: jax.random.permutation(one_key, CACHE))(jax.random.split(key_slot, columns * owners)).astype(jnp.int32)
    slot_perm = slot_perm.reshape(columns, owners, CACHE)
    slot_column = slot_perm[column_index[:, None], column_major, ranking]
    slot_grid = slot_column.reshape(columns, owners, per_device).transpose(1, 0, 2)
    return (owner_grid.reshape(-1).astype(jnp.int32), slot_grid.reshape(-1).astype(jnp.int32))


def draw_hash_owner(key, part):
    return owner_table(key)[0]


def draw_cache_slot(key, part):
    return owner_table(key)[1]


def with_ends(drawn, rng, smallest, largest):
    extent = drawn.shape
    index_at = [jax.random.randint(jax.random.fold_in(rng, axis), (), 0, extent[axis]) for axis in range(len(extent))]
    drawn = drawn.at[tuple(index_at)].set(smallest)
    longest = extent.index(max(extent))
    index_at[longest] = (index_at[longest] + 1) % extent[longest]
    return drawn.at[tuple(index_at)].set(largest)


def level_of(rng, dims, cuts, smallest, high):
    level, own = 1.0, jax.random.fold_in(rng, 6)
    for axis_at, blocks in cuts:
        draws = jnp.exp(jax.random.uniform(jax.random.fold_in(own, axis_at), (blocks,), jnp.float32, smallest / len(cuts), high / len(cuts)))
        level = level * jnp.repeat(draws, dims[axis_at] // blocks).reshape([-1 if axis == axis_at else 1 for axis in range(len(dims))])
    return level


def gaussian(own_key, shape, deviation, reach, shards=(), kind=jnp.bfloat16):
    array = jax.random.normal(own_key, shape, jnp.float32) * deviation
    if len(shards) > 0:
        array = level_of(own_key, shape, shards, -0.22, 0.18) * array
    return jnp.clip(array, min=-reach, max=reach).astype(kind)


def setup_inputs(seed: int = 0, part: int = 0) -> dict:
    streams_of = jax.random.split(jax.random.key(seed), 15)
    part_keys = jax.random.split(jax.random.fold_in(streams_of[14], part), 15)
    tokens = gaussian(part_keys[0], (STEPS, USERS, EV, D), 1.0, 6.0, ((1, 16),))
    in_weight = gaussian(streams_of[1], (D, CONV_CH), D ** -0.5, 0.125, ((0, 16),))
    dt_weight = gaussian(streams_of[2], (D, HEADS), D ** -0.5, 0.125, ((0, 16),))
    conv_weight = gaussian(streams_of[3], (KCONV, CONV_CH), KCONV ** -0.5, 3.0, (), jnp.float32)
    conv_bias = gaussian(streams_of[4], (CONV_CH,), 0.5, 3.0, (), jnp.float32)
    dt_bias = jnp.clip(jax.random.uniform(streams_of[5], (HEADS,), jnp.float32, -2.0, 1.0), -2.0, 1.0)
    decay_rate = jnp.clip(jnp.exp(jax.random.uniform(streams_of[6], (HEADS,), jnp.float32, math.log(0.004), math.log(0.3))), 0.004, 0.3)
    skip_gain = jnp.clip(jax.random.uniform(streams_of[7], (HEADS,), jnp.float32, 0.5, 1.5), 0.5, 1.5)
    norm_gain = jnp.clip(1.0 + 0.1 * jax.random.normal(streams_of[8], (INNER,), jnp.float32), 0.5, 1.5)
    state_cache = gaussian(part_keys[9], (SLOTS, HEADS, HEAD_DIM * STATE), 1.0, 6.0, ((0, 16),))
    conv_cache = gaussian(part_keys[10], (SLOTS, KCONV - 1, CONV_CH), 1.0, 6.0, ((0, 16),))
    hash_owner = draw_hash_owner(jax.random.fold_in(jax.random.fold_in(streams_of[14], part), 71), part)
    cache_slot = draw_cache_slot(jax.random.fold_in(jax.random.fold_in(streams_of[14], part), 71), part)
    event_counts = with_ends(jax.random.randint(part_keys[13], (STEPS, USERS), 1, EV + 1), jax.random.fold_in(part_keys[13], 1), 1, EV).astype(jnp.int32)
    return {"tokens": tokens, "in_weight": in_weight, "dt_weight": dt_weight, "conv_weight": conv_weight, "conv_bias": conv_bias, "dt_bias": dt_bias, "decay_rate": decay_rate, "skip_gain": skip_gain, "norm_gain": norm_gain, "state_cache": state_cache, "conv_cache": conv_cache, "hash_owner": hash_owner, "cache_slot": cache_slot, "event_counts": event_counts}


def advance(projected, dt_raw, counts, state, window, conv_weight, conv_bias, dt_bias, decay_rate, skip_gain, norm_gain):
    users = projected.shape[0]
    length = projected.shape[1]
    kernel = conv_weight.shape[0]
    extended = jnp.concatenate([window, projected], axis=1)
    ext_float = extended.astype(jnp.float32)
    conv_sum = conv_bias + conv_weight[0] * ext_float[:, 0:length]
    for tap in range(1, kernel):
        conv_sum = conv_sum + conv_weight[tap] * ext_float[:, tap:tap + length]
    active = jax.nn.silu(conv_sum)
    inner = active.shape[-1] - 2 * STATE
    inputs = active[..., :inner].reshape(users, length, HEADS, HEAD_DIM)
    write_vec = active[..., inner:inner + STATE]
    read_vec = active[..., inner + STATE:]
    positions = jnp.arange(length, dtype=jnp.int32)
    valid = (positions[None, :] < counts[:, None]).astype(jnp.float32)
    step_size = jax.nn.softplus(dt_raw.astype(jnp.float32) + dt_bias) * valid[:, :, None]
    cumulative = jnp.cumsum(-decay_rate * step_size, axis=1)
    total_log = cumulative[:, -1]
    weighting = jnp.exp(total_log[:, None, :] - cumulative) * step_size
    weighted = weighting[..., None] * inputs
    update = jnp.einsum('uthp,utn->uhpn', weighted, write_vec, precision=lax.Precision.HIGHEST)
    new_state = jnp.exp(total_log)[:, :, None, None] * state + update
    last_pick = (positions[None, :] == counts[:, None] - 1).astype(jnp.float32)
    last_input = jnp.einsum('ut,uthp->uhp', last_pick, inputs, precision=lax.Precision.HIGHEST)
    last_read = jnp.einsum('ut,utn->un', last_pick, read_vec, precision=lax.Precision.HIGHEST)
    mixed = lax.optimization_barrier(jnp.sum(new_state * last_read[:, None, None, :], axis=-1))
    mixed = (mixed + skip_gain[:, None] * last_input).reshape(users, -1)
    inv_rms = lax.rsqrt(lax.optimization_barrier(jnp.mean(mixed * mixed, axis=-1, keepdims=True)) + 1e-05)
    result = (mixed * inv_rms * norm_gain).astype(jnp.bfloat16)
    window_rows = counts[:, None] + jnp.arange(kernel - 1, dtype=jnp.int32)[None, :]
    new_window = jnp.take_along_axis(extended, window_rows[:, :, None], axis=1)
    return (result, new_state, new_window)

def reference(tokens, in_weight, dt_weight, conv_weight, conv_bias, dt_bias, decay_rate, skip_gain, norm_gain, state_cache, conv_cache, hash_owner, cache_slot, event_counts):
    blocks = N_REQ * N_FSDP
    user_index = jnp.arange(USERS, dtype=jnp.int32)
    column = user_index // USERS_DEV % N_FSDP
    cache_row = ((hash_owner * N_FSDP + column) * CACHE + cache_slot).astype(jnp.int32)
    width = in_weight.shape[1]

    def one_device(block):
        start = (block * USERS_DEV).astype(jnp.int32)
        tok_block = lax.dynamic_slice_in_dim(tokens, start, USERS_DEV, 1)
        count_block = lax.dynamic_slice_in_dim(event_counts, start, USERS_DEV, 1)
        rows_block = lax.dynamic_slice_in_dim(cache_row, start, USERS_DEV, 0)
        flat_tokens = tok_block.reshape(-1, D)
        proj_in = jnp.dot(flat_tokens, in_weight, preferred_element_type=jnp.float32).astype(jnp.bfloat16)
        proj_in = proj_in.reshape(STEPS, USERS_DEV, EV, width)
        proj_dt = jnp.dot(flat_tokens, dt_weight, preferred_element_type=jnp.float32).astype(jnp.bfloat16)
        proj_dt = proj_dt.reshape(STEPS, USERS_DEV, EV, HEADS)
        state = state_cache[rows_block].astype(jnp.float32).reshape(USERS_DEV, HEADS, HEAD_DIM, STATE)
        window = conv_cache[rows_block]
        results = []
        for step in range(STEPS):
            result, state, window = advance(proj_in[step], proj_dt[step], count_block[step], state, window, conv_weight, conv_bias, dt_bias, decay_rate, skip_gain, norm_gain)
            results.append(result)
        final_state = state.reshape(USERS_DEV, HEADS, HEAD_DIM * STATE).astype(jnp.bfloat16)
        return (jnp.stack(results), final_state, window)
    outputs, states, windows = lax.map(one_device, jnp.arange(blocks, dtype=jnp.int32))
    user_vectors = outputs.transpose(1, 0, 2, 3).reshape(STEPS, USERS, -1)
    new_states = state_cache.at[cache_row].set(states.reshape(USERS, HEADS, HEAD_DIM * STATE))
    new_windows = conv_cache.at[cache_row].set(windows.reshape(USERS, KCONV - 1, width))
    return (user_vectors, new_states, new_windows)
```

```python
import jax
import jax.numpy as jnp
from jax import lax
from jax.experimental import pallas as pl
from jax.experimental.pallas import tpu as pltpu
from jax.sharding import PartitionSpec as P

HEADS = 64
HEAD_DIM = 64
STATE = 64
STEPS = 2
GROUP = 8


def state_kernel(x_ref, b_ref, r_ref, decay_ref, h_ref, new_ref, read_ref):
    depth = x_ref.shape[2] // (HEAD_DIM // GROUP)
    wide = GROUP * STATE
    outs = r_ref.shape[2]
    write = b_ref[0]
    read = r_ref[0]
    decay = decay_ref[0]
    for q in range(HEAD_DIM // GROUP):
        old = h_ref[0, :, q * wide : (q + 1) * wide]
        update = jnp.dot(
            x_ref[0, :, q * depth : (q + 1) * depth], write, preferred_element_type=jnp.float32
        )
        new_ref[0, :, q * wide : (q + 1) * wide] = (
            decay * old.astype(jnp.float32) + update
        ).astype(jnp.bfloat16)
        read_ref[0, :, q * outs : (q + 1) * outs] = jnp.dot(
            old, read, preferred_element_type=jnp.float32
        )


def update_states(x_rows, b_blocks, r_blocks, decay, state):
    cached = state.shape[0]
    outs = r_blocks.shape[2] * (HEAD_DIM // GROUP)

    def spec(array):
        return pl.BlockSpec((1,) + array.shape[1:], lambda u: (u, 0, 0))

    return pl.pallas_call(
        state_kernel,
        grid=(cached,),
        in_specs=[spec(x_rows), spec(b_blocks), spec(r_blocks), spec(decay), spec(state)],
        out_specs=[spec(state), pl.BlockSpec((1, HEADS, outs), lambda u: (u, 0, 0))],
        out_shape=[
            jax.ShapeDtypeStruct(state.shape, jnp.bfloat16),
            jax.ShapeDtypeStruct((cached, HEADS, outs), jnp.float32),
        ],
    )(x_rows, b_blocks, r_blocks, decay, state)


def advance(projected, dt_raw, counts, state, window, params):
    conv_weight, conv_bias, dt_bias, decay_rate, skip_gain, norm_gain = params
    cached, steps, length, width = projected.shape
    kernel = conv_weight.shape[0]
    inner = HEADS * HEAD_DIM
    positions = jnp.arange(length, dtype=jnp.int32)
    row_of = jnp.arange(length + kernel - 1, dtype=jnp.int32)
    actives = []
    for step in range(steps):
        extended = jnp.concatenate([window, projected[:, step]], axis=1)
        ext_float = extended.astype(jnp.float32)
        conv_sum = conv_bias + conv_weight[0] * ext_float[:, 0:length]
        for tap in range(1, kernel):
            conv_sum = conv_sum + conv_weight[tap] * ext_float[:, tap : tap + length]
        actives.append(jax.nn.silu(conv_sum))
        wanted = counts[:, step, None] + jnp.arange(kernel - 1, dtype=jnp.int32)[None, :]
        pick = (wanted[:, :, None] == row_of[None, None, :]).astype(jnp.bfloat16)
        window = jnp.einsum(
            "uwr,urc->uwc", pick, extended, preferred_element_type=jnp.float32
        ).astype(jnp.bfloat16)
    active = jnp.stack(actives, axis=1)
    inputs = active[..., :inner]
    write_vec = active[..., inner : inner + STATE]
    read_vec = active[..., inner + STATE :]
    valid = (positions[None, None, :] < counts[:, :, None]).astype(jnp.float32)
    step_size = jax.nn.softplus(dt_raw.astype(jnp.float32) + dt_bias) * valid[..., None]
    cumulative = jnp.cumsum(-decay_rate * step_size, axis=2)
    total_log = cumulative[:, :, -1]
    weighting = jnp.exp(total_log[:, :, None, :] - cumulative) * step_size
    decay_both = jnp.exp(total_log[:, 0] + total_log[:, 1])
    weight_end = jnp.stack(
        [weighting[:, 0] * jnp.exp(total_log[:, 1])[:, None, :], weighting[:, 1]], axis=1
    )
    last_pick = (positions[None, None, :] == counts[:, :, None] - 1).astype(jnp.float32)
    last_read = jnp.sum(last_pick[..., None] * read_vec, axis=2)

    events = steps * length
    x_heads = inputs.reshape(cached, events, HEADS, HEAD_DIM)
    weighted = x_heads * weight_end.reshape(cached, events, HEADS)[..., None]
    x_rows = weighted.astype(jnp.bfloat16).transpose(0, 2, 3, 1)
    x_rows = x_rows.reshape(cached, HEADS, HEAD_DIM * events)
    eye = jnp.eye(GROUP, dtype=jnp.bfloat16)
    b_all = write_vec.reshape(cached, events, STATE).astype(jnp.bfloat16)
    b_blocks = (eye[None, :, None, :, None] * b_all[:, None, :, None, :]).reshape(
        cached, GROUP * events, GROUP * STATE
    )
    r_low = last_read.astype(jnp.bfloat16)
    r_blocks = (
        eye[None, :, None, None, :] * r_low.transpose(0, 2, 1)[:, None, :, :, None]
    ).reshape(cached, GROUP * STATE, steps * GROUP)
    new_state, read_old = update_states(x_rows, b_blocks, r_blocks, decay_both[:, :, None], state)
    read_old = read_old.reshape(cached, HEADS, HEAD_DIM // GROUP, steps, GROUP)
    read_old = read_old.transpose(0, 3, 1, 2, 4).reshape(cached, steps, HEADS, HEAD_DIM)
    gram = jnp.sum(
        write_vec.reshape(cached, 1, events, STATE) * last_read[:, :, None, :], axis=-1
    )
    zero = jnp.zeros_like(weighting[:, 0])
    weight_first = jnp.concatenate([weighting[:, 0], zero], axis=1)
    weight_both = weight_end.reshape(cached, events, HEADS)
    coef = jnp.stack([weight_first, weight_both], axis=1) * gram[..., None]
    placed = (last_pick[:, None] * jnp.eye(steps, dtype=jnp.float32)[None, :, :, None]).reshape(
        cached, steps, events
    )
    coef = coef + placed[..., None] * skip_gain
    from_old = jnp.stack([jnp.exp(total_log[:, 0]), decay_both], axis=1)
    spread = jnp.repeat(coef, HEAD_DIM, axis=-1)
    mixed = jnp.sum(spread * inputs.reshape(cached, 1, events, inner), axis=2)
    mixed = mixed + (from_old[..., None] * read_old).reshape(cached, steps, inner)
    inv_rms = lax.rsqrt(jnp.mean(mixed * mixed, axis=-1, keepdims=True) + 1e-05)
    result = (mixed * inv_rms * norm_gain).astype(jnp.bfloat16)
    return (result, new_state, window)


def on_device(
    tokens,
    in_weight,
    dt_weight,
    conv_weight,
    conv_bias,
    dt_bias,
    decay_rate,
    skip_gain,
    norm_gain,
    state_cache,
    conv_cache,
    hash_owner,
    cache_slot,
    event_counts,
):
    owners = lax.axis_size("req")
    users = tokens.shape[1]
    length = tokens.shape[2]
    model = tokens.shape[3]
    cached = state_cache.shape[0]
    capacity = max(2, (2 * users + owners - 1) // owners)
    params = (conv_weight, conv_bias, dt_bias, decay_rate, skip_gain, norm_gain)
    both = jnp.concatenate([in_weight, dt_weight], axis=1)
    full = lax.all_gather(both, ("req", "fsdp"), axis=0, tiled=True)
    matches = (hash_owner[:, None] == jnp.arange(owners, dtype=jnp.int32)[None, :]).astype(
        jnp.int32
    )
    ranking = jnp.sum((jnp.cumsum(matches, axis=0) - matches) * matches, axis=1)
    requests = jnp.full((owners, capacity), -1, jnp.int32).at[hash_owner, ranking].set(cache_slot)
    count_table = (
        jnp.zeros((owners, capacity, STEPS), jnp.int32).at[hash_owner, ranking].set(event_counts.T)
    )
    orders = jnp.concatenate([requests[:, :, None], count_table], axis=2)
    arrived = lax.all_to_all(orders, "req", split_axis=0, concat_axis=0, tiled=True)
    flat_slots = arrived[:, :, 0].reshape(-1)
    item_counts = arrived[:, :, 1:].reshape(-1, STEPS)
    live_slots = flat_slots >= 0
    safe_slots = jnp.clip(flat_slots, 0, cached - 1)
    target_rows = jnp.where(live_slots, flat_slots, cached)
    cache_counts = (
        jnp.zeros((cached, STEPS), jnp.int32).at[target_rows].set(item_counts, mode="drop")
    )
    send_rows = (
        jnp.zeros((owners, capacity, STEPS, length, model), jnp.bfloat16)
        .at[hash_owner, ranking]
        .set(tokens.transpose(1, 0, 2, 3))
    )
    came_rows = lax.all_to_all(send_rows, "req", split_axis=0, concat_axis=0, tiled=True)
    cache_tokens = (
        jnp.zeros((cached, STEPS, length, model), jnp.bfloat16)
        .at[target_rows]
        .set(came_rows.reshape(-1, STEPS, length, model), mode="drop")
    )
    width = in_weight.shape[1]
    proj = jnp.dot(
        cache_tokens.reshape(-1, model), full, preferred_element_type=jnp.float32
    ).astype(jnp.bfloat16)
    proj = proj.reshape(cached, STEPS, length, -1)
    stacked, new_states, work_window = advance(
        proj[..., :width], proj[..., width:], cache_counts, state_cache, conv_cache, params
    )
    item_result = stacked[safe_slots].reshape(owners, capacity, STEPS, -1)
    returned = lax.all_to_all(item_result, "req", split_axis=0, concat_axis=0, tiled=True)
    user_vectors = returned[hash_owner, ranking].transpose(1, 0, 2)
    return (user_vectors, new_states, work_window)


def solution(mesh):
    in_specs = (
        P(None, ("groups", "req", "fsdp"), None, None),
        P(("req", "fsdp"), None),
        P(("req", "fsdp"), None),
        P(),
        P(),
        P(),
        P(),
        P(),
        P(),
        P(("groups", "req", "fsdp"), None, None),
        P(("groups", "req", "fsdp"), None, None),
        P(("groups", "req", "fsdp")),
        P(("groups", "req", "fsdp")),
        P(None, ("groups", "req", "fsdp")),
    )
    out_specs = (
        P(None, ("groups", "req", "fsdp"), None),
        P(("groups", "req", "fsdp"), None, None),
        P(("groups", "req", "fsdp"), None, None),
    )
    return jax.shard_map(
        on_device, mesh=mesh, in_specs=in_specs, out_specs=out_specs, check_vma=False
    )
```

```python
import functools

import jax
import jax.numpy as jnp
from jax import lax
from jax.experimental import pallas as pl
from jax.experimental.pallas import tpu as pltpu
from jax.sharding import PartitionSpec as P

HEADS = 64
HEAD_DIM = 64
STATE = 64
STEPS = 2
GROUP = 8


def state_kernel(x_ref, b_ref, r_ref, decay_ref, h_ref, new_ref, read_ref):
    depth = x_ref.shape[2] // (HEAD_DIM // GROUP)
    wide = GROUP * STATE
    outs = r_ref.shape[2]
    write = b_ref[0]
    read = r_ref[0]
    decay = decay_ref[0]
    for q in range(HEAD_DIM // GROUP):
        old = h_ref[0, :, q * wide : (q + 1) * wide]
        update = jnp.dot(
            x_ref[0, :, q * depth : (q + 1) * depth], write, preferred_element_type=jnp.float32
        )
        new_ref[0, :, q * wide : (q + 1) * wide] = (
            decay * old.astype(jnp.float32) + update
        ).astype(jnp.bfloat16)
        read_ref[0, :, q * outs : (q + 1) * outs] = jnp.dot(
            old, read, preferred_element_type=jnp.float32
        )


def update_states(x_rows, b_blocks, r_blocks, decay, state):
    cached = state.shape[0]
    outs = r_blocks.shape[2] * (HEAD_DIM // GROUP)

    def spec(array):
        return pl.BlockSpec((1,) + array.shape[1:], lambda u: (u, 0, 0))

    return pl.pallas_call(
        state_kernel,
        grid=(cached,),
        in_specs=[spec(x_rows), spec(b_blocks), spec(r_blocks), spec(decay), spec(state)],
        out_specs=[spec(state), pl.BlockSpec((1, HEADS, outs), lambda u: (u, 0, 0))],
        out_shape=[
            jax.ShapeDtypeStruct(state.shape, jnp.bfloat16),
            jax.ShapeDtypeStruct((cached, HEADS, outs), jnp.float32),
        ],
    )(x_rows, b_blocks, r_blocks, decay, state)


def advance(projected, dt_raw, counts, state, window, params):
    conv_weight, conv_bias, dt_bias, decay_rate, skip_gain, norm_gain = params
    cached, steps, length, width = projected.shape
    kernel = conv_weight.shape[0]
    inner = HEADS * HEAD_DIM
    positions = jnp.arange(length, dtype=jnp.int32)
    row_of = jnp.arange(length + kernel - 1, dtype=jnp.int32)
    actives = []
    for step in range(steps):
        extended = jnp.concatenate([window, projected[:, step]], axis=1)
        ext_float = extended.astype(jnp.float32)
        conv_sum = conv_bias + conv_weight[0] * ext_float[:, 0:length]
        for tap in range(1, kernel):
            conv_sum = conv_sum + conv_weight[tap] * ext_float[:, tap : tap + length]
        actives.append(jax.nn.silu(conv_sum))
        wanted = counts[:, step, None] + jnp.arange(kernel - 1, dtype=jnp.int32)[None, :]
        pick = (wanted[:, :, None] == row_of[None, None, :]).astype(jnp.bfloat16)
        window = jnp.einsum(
            "uwr,urc->uwc", pick, extended, preferred_element_type=jnp.float32
        ).astype(jnp.bfloat16)
    active = jnp.stack(actives, axis=1)
    inputs = active[..., :inner]
    write_vec = active[..., inner : inner + STATE]
    read_vec = active[..., inner + STATE :]
    valid = (positions[None, None, :] < counts[:, :, None]).astype(jnp.float32)
    step_size = jax.nn.softplus(dt_raw.astype(jnp.float32) + dt_bias) * valid[..., None]
    cumulative = jnp.cumsum(-decay_rate * step_size, axis=2)
    total_log = cumulative[:, :, -1]
    weighting = jnp.exp(total_log[:, :, None, :] - cumulative) * step_size
    decay_both = jnp.exp(total_log[:, 0] + total_log[:, 1])
    weight_end = jnp.stack(
        [weighting[:, 0] * jnp.exp(total_log[:, 1])[:, None, :], weighting[:, 1]], axis=1
    )
    last_pick = (positions[None, None, :] == counts[:, :, None] - 1).astype(jnp.float32)
    last_read = jnp.sum(last_pick[..., None] * read_vec, axis=2)

    events = steps * length
    x_heads = inputs.reshape(cached, events, HEADS, HEAD_DIM)
    weighted = x_heads * weight_end.reshape(cached, events, HEADS)[..., None]
    x_rows = weighted.astype(jnp.bfloat16).transpose(0, 2, 3, 1)
    x_rows = x_rows.reshape(cached, HEADS, HEAD_DIM * events)
    eye = jnp.eye(GROUP, dtype=jnp.bfloat16)
    b_all = write_vec.reshape(cached, events, STATE).astype(jnp.bfloat16)
    b_blocks = (eye[None, :, None, :, None] * b_all[:, None, :, None, :]).reshape(
        cached, GROUP * events, GROUP * STATE
    )
    r_low = last_read.astype(jnp.bfloat16)
    r_blocks = (
        eye[None, :, None, None, :] * r_low.transpose(0, 2, 1)[:, None, :, :, None]
    ).reshape(cached, GROUP * STATE, steps * GROUP)
    new_state, read_old = update_states(x_rows, b_blocks, r_blocks, decay_both[:, :, None], state)
    read_old = read_old.reshape(cached, HEADS, HEAD_DIM // GROUP, steps, GROUP)
    read_old = read_old.transpose(0, 3, 1, 2, 4).reshape(cached, steps, HEADS, HEAD_DIM)
    gram = jnp.sum(
        write_vec.reshape(cached, 1, events, STATE) * last_read[:, :, None, :], axis=-1
    )
    zero = jnp.zeros_like(weighting[:, 0])
    weight_first = jnp.concatenate([weighting[:, 0], zero], axis=1)
    weight_both = weight_end.reshape(cached, events, HEADS)
    coef = jnp.stack([weight_first, weight_both], axis=1) * gram[..., None]
    placed = (last_pick[:, None] * jnp.eye(steps, dtype=jnp.float32)[None, :, :, None]).reshape(
        cached, steps, events
    )
    coef = coef + placed[..., None] * skip_gain
    from_old = jnp.stack([jnp.exp(total_log[:, 0]), decay_both], axis=1)
    spread = jnp.repeat(coef, HEAD_DIM, axis=-1)
    mixed = jnp.sum(spread * inputs.reshape(cached, 1, events, inner), axis=2)
    mixed = mixed + (from_old[..., None] * read_old).reshape(cached, steps, inner)
    inv_rms = lax.rsqrt(jnp.mean(mixed * mixed, axis=-1, keepdims=True) + 1e-05)
    result = (mixed * inv_rms * norm_gain).astype(jnp.bfloat16)
    return (result, new_state, window)


MESH = pl.DeviceIdType.MESH


def project_kernel(
    sizes, tok_ref, w_ref, meta_ref, out_ref, meta_out,
    tokbuf, wbuf, acc, pbuf, sendbuf, recvbuf, metabuf,
    local_sem, tok_send, tok_recv, meta_send, meta_recv, plane_send, w_recv,
    up_send, down_send, row_send, row_recv,
):
    groups, owners, line, cached, users, length = sizes
    plane = groups * owners
    g = lax.axis_index("groups")
    r = lax.axis_index("req")
    f = lax.axis_index("fsdp")
    me = g * owners + r
    rows = tok_ref.shape[1]
    depth = w_ref.shape[0]
    wide = wbuf.shape[2]
    has_up = f < line - 1
    has_down = f > 0

    def at(q):
        return {"groups": q // owners, "req": lax.rem(q, owners), "fsdp": f}

    up = {"groups": g, "req": r, "fsdp": f + 1}
    down = {"groups": g, "req": r, "fsdp": f - 1}

    barrier = pltpu.get_barrier_semaphore()
    for p in range(1, plane):
        pl.semaphore_signal(
            barrier, inc=1, device_id=at(lax.rem(me + p, plane)), device_id_type=MESH
        )

    @pl.when(has_up)
    def _():
        pl.semaphore_signal(barrier, inc=1, device_id=up, device_id_type=MESH)

    @pl.when(has_down)
    def _():
        pl.semaphore_signal(barrier, inc=1, device_id=down, device_id_type=MESH)

    own_w = pltpu.make_async_copy(
        w_ref.at[:, pl.ds(pl.multiple_of(me * wide, 128), wide)],
        wbuf.at[f, pl.ds(pl.multiple_of(r * depth, depth), depth)],
        local_sem.at[0],
    )
    own_w.start()
    own_tok = pltpu.make_async_copy(tok_ref, tokbuf.at[me], local_sem.at[1])
    own_tok.start()
    own_meta = pltpu.make_async_copy(meta_ref, metabuf.at[me], local_sem.at[2])
    own_meta.start()
    pl.semaphore_wait(
        barrier, plane - 1 + has_up.astype(jnp.int32) + has_down.astype(jnp.int32)
    )

    def plane_copy(p):
        to = lax.rem(r + p, owners)
        q = g * owners + to
        return pltpu.make_async_remote_copy(
            src_ref=w_ref.at[:, pl.ds(pl.multiple_of(q * wide, 128), wide)],
            dst_ref=wbuf.at[f, pl.ds(pl.multiple_of(r * depth, depth), depth)],
            send_sem=plane_send.at[p],
            recv_sem=w_recv.at[f, r],
            device_id=at(q),
            device_id_type=MESH,
        )

    def line_copy(piece_f, piece_r, sems, target):
        block = wbuf.at[piece_f, pl.ds(pl.multiple_of(piece_r * depth, depth), depth)]
        return pltpu.make_async_remote_copy(
            src_ref=block,
            dst_ref=block,
            send_sem=sems.at[piece_f, piece_r],
            recv_sem=w_recv.at[piece_f, piece_r],
            device_id=target,
            device_id_type=MESH,
        )

    def peer_copy(src, dst, sends, recvs, p):
        return pltpu.make_async_remote_copy(
            src_ref=src,
            dst_ref=dst,
            send_sem=sends.at[p],
            recv_sem=recvs.at[p],
            device_id=at(lax.rem(me + p, plane)),
            device_id_type=MESH,
        )

    def tok_copy(p):
        return peer_copy(tok_ref, tokbuf.at[me], tok_send, tok_recv, p)

    def meta_copy(p):
        return peer_copy(meta_ref, metabuf.at[me], meta_send, meta_recv, p)

    def row_copy(p):
        q = lax.rem(me + p, plane)
        return peer_copy(sendbuf.at[q], recvbuf.at[me], row_send, row_recv, p)

    def send_up(piece_f, piece_r):
        @pl.when(has_up)
        def _():
            line_copy(piece_f, piece_r, up_send, up).start()

    def send_down(piece_f, piece_r):
        @pl.when(has_down)
        def _():
            line_copy(piece_f, piece_r, down_send, down).start()

    for p in range(1, owners):
        plane_copy(p).start()
    own_w.wait()
    send_up(f, r)
    send_down(f, r)
    for p in range(1, plane):
        meta_copy(p).start()
        tok_copy(p).start()
    for p in range(1, owners):
        came = lax.rem(r + owners - p, owners)
        line_copy(f, came, up_send, up).wait_recv()
        send_up(f, came)
        send_down(f, came)
    own_tok.wait()
    own_meta.wait()
    for p in range(1, plane):
        tok_copy(p).wait_recv()

    def partial_product(piece):
        return jnp.dot(
            tokbuf[:, piece].reshape(plane * rows, owners * depth),
            wbuf[piece],
            preferred_element_type=jnp.float32,
        )

    acc[...] = partial_product(f)
    for d in range(1, line):

        @pl.when(f - d >= 0)
        def _():
            for p in range(owners):
                piece_r = lax.rem(r + owners - p, owners)
                line_copy(f - d, piece_r, up_send, up).wait_recv()
                send_up(f - d, piece_r)

        @pl.when(f + d < line)
        def _():
            for p in range(owners):
                piece_r = lax.rem(r + owners - p, owners)
                line_copy(f + d, piece_r, down_send, down).wait_recv()
                send_down(f + d, piece_r)

        @pl.when(f - d >= 0)
        def _():
            acc[...] += partial_product(f - d)

        @pl.when(f + d < line)
        def _():
            acc[...] += partial_product(f + d)

    pbuf[...] = acc[...].astype(jnp.bfloat16).reshape(plane, rows, wide)
    for p in range(1, plane):
        meta_copy(p).wait_recv()

    items = cached * STEPS * length
    row = lax.broadcasted_iota(jnp.int32, (items, rows), 0)
    col = lax.broadcasted_iota(jnp.int32, (items, rows), 1)
    slot = row // (STEPS * length)
    same_event = lax.rem(row, STEPS * length) == (
        col // (users * length) * length + lax.rem(col, length)
    )

    def rows_for(p):
        q = lax.rem(me + p, plane)
        base = q // owners * owners
        wanted = lax.rem(q, owners) * cached + slot
        total = jnp.zeros((items, wide), jnp.float32)
        for source in range(owners):
            code = metabuf[base + source][0:1, 0:rows]
            pick = jnp.where((code == wanted) & same_event, 1.0, 0.0).astype(jnp.bfloat16)
            total = total + jnp.dot(
                pick, pbuf[base + source], preferred_element_type=jnp.float32
            )
        return total.astype(jnp.bfloat16)

    @pl.loop(1, plane)
    def _(p):
        sendbuf[lax.rem(me + p, plane)] = rows_for(p)
        row_copy(p).start()

    recvbuf[me] = rows_for(0)
    meta_out[...] = metabuf[...]
    for p in range(1, plane):
        row_copy(p).wait_recv()
    for q in range(plane):
        out_ref[:, q * wide : (q + 1) * wide] = recvbuf[q]
    for p in range(1, plane):
        tok_copy(p).wait_send()
        meta_copy(p).wait_send()
        row_copy(p).wait_send()
    for p in range(1, owners):
        plane_copy(p).wait_send()
    for d in range(line):

        @pl.when((f - d >= 0) & has_up)
        def _():
            for piece_r in range(owners):
                line_copy(f - d, piece_r, up_send, up).wait_send()

        @pl.when((f + d < line) & has_down)
        def _():
            for piece_r in range(owners):
                line_copy(f + d, piece_r, down_send, down).wait_send()


def project(tokens, weight, meta, sizes):
    groups, owners, line, cached, users, length = sizes
    plane = groups * owners
    rows = tokens.shape[1]
    depth = weight.shape[0]
    wide = weight.shape[1] // plane
    items = cached * STEPS * length
    dma = pltpu.SemaphoreType.DMA
    vmem = pl.BlockSpec(memory_space=pltpu.VMEM)
    return pl.pallas_call(
        functools.partial(project_kernel, sizes),
        in_specs=[vmem] * 3,
        out_specs=[vmem] * 2,
        out_shape=[
            jax.ShapeDtypeStruct((items, plane * wide), jnp.bfloat16),
            jax.ShapeDtypeStruct((plane,) + meta.shape, jnp.int32),
        ],
        scratch_shapes=[
            pltpu.VMEM((plane,) + tokens.shape, jnp.bfloat16),
            pltpu.VMEM((line, owners * depth, wide), jnp.bfloat16),
            pltpu.VMEM((plane * rows, wide), jnp.float32),
            pltpu.VMEM((plane, rows, wide), jnp.bfloat16),
            pltpu.VMEM((plane, items, wide), jnp.bfloat16),
            pltpu.VMEM((plane, items, wide), jnp.bfloat16),
            pltpu.VMEM((plane,) + meta.shape, jnp.int32),
            dma((3,)),
            dma((plane,)),
            dma((plane,)),
            dma((plane,)),
            dma((plane,)),
            dma((owners,)),
            dma((line, owners)),
            dma((line, owners)),
            dma((line, owners)),
            dma((plane,)),
            dma((plane,)),
        ],
        compiler_params=pltpu.CompilerParams(
            collective_id=0, has_side_effects=True, vmem_limit_bytes=56 * 1024 * 1024
        ),
    )(tokens, weight, meta)


def on_device(
    tokens,
    in_weight,
    dt_weight,
    conv_weight,
    conv_bias,
    dt_bias,
    decay_rate,
    skip_gain,
    norm_gain,
    state_cache,
    conv_cache,
    hash_owner,
    cache_slot,
    event_counts,
):
    owners = lax.axis_size("req")
    users = tokens.shape[1]
    length = tokens.shape[2]
    model = tokens.shape[3]
    cached = state_cache.shape[0]
    capacity = max(2, (2 * users + owners - 1) // owners)
    params = (conv_weight, conv_bias, dt_bias, decay_rate, skip_gain, norm_gain)
    groups = lax.axis_size("groups")
    line = lax.axis_size("fsdp")
    plane = groups * owners
    width = in_weight.shape[1]
    depth = in_weight.shape[0]
    wide = -(-(width + HEADS) // (128 * plane)) * 128
    both = jnp.concatenate(
        [
            in_weight,
            dt_weight,
            jnp.zeros((depth, plane * wide - width - HEADS), jnp.bfloat16),
        ],
        axis=1,
    )
    rows = STEPS * users * length
    tok = tokens.reshape(rows, owners, line, depth).transpose(2, 0, 1, 3)
    tok = tok.reshape(line, rows, owners * depth)

    def per_row(values):
        return jnp.repeat(values, length, axis=-1).reshape(-1)

    code = hash_owner * cached + cache_slot
    meta = jnp.stack(
        [per_row(jnp.stack([code] * STEPS)), per_row(event_counts)], axis=0
    ).astype(jnp.int32)
    meta = jnp.pad(meta, ((0, 6), (0, (-rows) % 128)), constant_values=-1)
    proj, all_meta = project(tok, both, meta, (groups, owners, line, cached, users, length))
    mine = lax.dynamic_slice_in_dim(all_meta, lax.axis_index("groups") * owners, owners, 0)
    mine = mine[:, :2, :rows].reshape(owners, 2, STEPS, users, length)[..., 0]
    codes = mine[:, 0, 0]
    came_counts = mine[:, 1]
    me = lax.axis_index("req")
    slots = jnp.arange(cached, dtype=jnp.int32)
    hit = codes[:, :, None] == me * cached + slots
    cache_counts = jnp.sum(
        hit[:, None].astype(jnp.int32) * came_counts[..., None], axis=(0, 2)
    ).T
    same = (codes[:, :, None] // cached == codes[:, None, :] // cached).astype(jnp.int32)
    before = jnp.tril(jnp.ones((users, users), jnp.int32), -1)
    ranks = jnp.sum(same * before, axis=2)
    turn = ranks[:, :, None] == jnp.arange(capacity, dtype=jnp.int32)
    route = jnp.sum(
        (turn[..., None] & hit[:, :, None, :]).astype(jnp.float32), axis=1
    ).astype(jnp.bfloat16)
    equal = (hash_owner[:, None] == hash_owner[None, :]).astype(jnp.int32)
    ranking = jnp.sum(equal * before, axis=1)
    proj = proj.reshape(cached, STEPS, length, -1)
    stacked, new_states, work_window = advance(
        proj[..., :width], proj[..., width : width + HEADS], cache_counts, state_cache, conv_cache, params
    )
    item_result = jnp.einsum(
        "ocs,sd->ocd",
        route,
        stacked.reshape(cached, -1),
        preferred_element_type=jnp.float32,
    )
    item_result = item_result.astype(jnp.bfloat16).reshape(owners, capacity, STEPS, -1)
    returned = lax.all_to_all(item_result, "req", split_axis=0, concat_axis=0, tiled=True)
    user_vectors = returned[hash_owner, ranking].transpose(1, 0, 2)
    return (user_vectors, new_states, work_window)


def solution(mesh):
    in_specs = (
        P(None, ("groups", "req", "fsdp"), None, None),
        P(("req", "fsdp"), None),
        P(("req", "fsdp"), None),
        P(),
        P(),
        P(),
        P(),
        P(),
        P(),
        P(("groups", "req", "fsdp"), None, None),
        P(("groups", "req", "fsdp"), None, None),
        P(("groups", "req", "fsdp")),
        P(("groups", "req", "fsdp")),
        P(None, ("groups", "req", "fsdp")),
    )
    out_specs = (
        P(None, ("groups", "req", "fsdp"), None),
        P(("groups", "req", "fsdp"), None, None),
        P(("groups", "req", "fsdp"), None, None),
    )
    return jax.shard_map(
        on_device, mesh=mesh, in_specs=in_specs, out_specs=out_specs, check_vma=False
    )
```

```python
import functools

import jax
import jax.numpy as jnp
from jax import lax
from jax.experimental import pallas as pl
from jax.experimental.pallas import tpu as pltpu
from jax.sharding import PartitionSpec as P

HEADS = 64
HEAD_DIM = 64
STATE = 64
STEPS = 2
GROUP = 8


def split_dot(value, picks):
    high = value.astype(jnp.bfloat16)
    low = (value - high.astype(jnp.float32)).astype(jnp.bfloat16)
    return jnp.dot(high, picks, preferred_element_type=jnp.float32) + jnp.dot(
        low, picks, preferred_element_type=jnp.float32
    )


def user_kernel(
    count_ref, proj_ref, window_ref, conv_ref, bias_ref, head_ref, gain_ref, expand_ref,
    place_ref, tile_ref, h_ref, out_ref, new_ref, window_out, flip_ref, read_ref,
):
    u = pl.program_id(0)
    taps = conv_ref.shape[0]
    width = conv_ref.shape[1]
    length = proj_ref.shape[0] // STEPS
    events = STEPS * length
    inner = HEADS * HEAD_DIM
    spans = HEAD_DIM // GROUP
    wide = GROUP * STATE
    lane = GROUP * events
    counts = [count_ref[u, step] for step in range(STEPS)]

    window = window_ref[0].astype(jnp.float32)
    ext_rows = lax.broadcasted_iota(jnp.int32, (length + taps - 1, width), 0)
    actives = []
    for step in range(STEPS):
        fresh = proj_ref[step * length : (step + 1) * length, 0:width].astype(jnp.float32)
        extended = jnp.concatenate([window, fresh], axis=0)
        conv_sum = bias_ref[...] + conv_ref[0:1] * extended[0:length]
        for tap in range(1, taps):
            conv_sum = conv_sum + conv_ref[tap : tap + 1] * extended[tap : tap + length]
        actives.append(conv_sum * jax.nn.sigmoid(conv_sum))
        window = jnp.concatenate(
            [
                jnp.sum(
                    jnp.where(ext_rows == counts[step] + w, extended, 0.0), axis=0, keepdims=True
                )
                for w in range(taps - 1)
            ],
            axis=0,
        )
    window_out[0] = window.astype(jnp.bfloat16)
    active = jnp.concatenate(actives, axis=0)
    inputs = active[:, 0:inner]
    both = active[:, inner:width]

    row = lax.broadcasted_iota(jnp.int32, (events, 128), 0)
    in_first = row < length
    limit = jnp.where(in_first, counts[0], length + counts[1])
    dt = proj_ref[:, width : width + 128].astype(jnp.float32) + head_ref[0:1]
    soft = jnp.maximum(dt, 0.0) + jnp.log1p(jnp.exp(-jnp.abs(dt)))
    step_size = jnp.where(row < limit, soft, 0.0)
    slope = -head_ref[1:2] * step_size
    one = slope[0:1]
    sums = [one]
    for t in range(1, events):
        one = slope[t : t + 1] + (0.0 if t == length else one)
        sums.append(one)
    cumulative = jnp.concatenate(sums, axis=0)
    total_0, total_1 = sums[length - 1], sums[events - 1]
    weight = jnp.exp(jnp.where(in_first, total_0, total_1) - cumulative) * step_size
    weight_end = jnp.where(in_first, jnp.exp(total_1), 1.0) * weight
    last = [
        (row == counts[0] - 1) & in_first,
        (row == length + counts[1] - 1) & (row >= length),
    ]
    reads = [jnp.sum(jnp.where(pick, both, 0.0), axis=0, keepdims=True) for pick in last]
    left = lax.broadcasted_iota(jnp.int32, (events, 128), 1) < STATE
    coefs = []
    for step in range(STEPS):
        turned = pltpu.roll(reads[step], STATE, 1)
        gram = jnp.sum(jnp.where(left, both * turned, 0.0), axis=1, keepdims=True)
        base = jnp.where(in_first, weight, 0.0) if step == 0 else weight_end
        coefs.append(base * gram + jnp.where(last[step], head_ref[2:3], 0.0))
    decay_0 = jnp.exp(total_0)
    decay_both = jnp.exp(total_0 + total_1)
    stacked = jnp.concatenate(
        [weight_end, coefs[0], coefs[1], decay_0, decay_both, jnp.zeros((6, 128), jnp.float32)],
        axis=0,
    )
    spread = split_dot(stacked, expand_ref[...])
    weighted = (inputs * spread[0:events]).astype(jnp.bfloat16)

    event_of = lax.rem(lax.broadcasted_iota(jnp.int32, (events, lane), 1), events)
    copies = (event_of == lax.broadcasted_iota(jnp.int32, (events, lane), 0)).astype(jnp.float32)
    flip_ref[...] = lax.dot_general(
        weighted,
        copies.astype(jnp.bfloat16),
        (((0,), (0,)), ((), ())),
        preferred_element_type=jnp.float32,
    ).reshape(HEADS, spans, GROUP, lane)
    own = (
        lax.broadcasted_iota(jnp.int32, (HEADS, GROUP, lane), 1)
        == lax.broadcasted_iota(jnp.int32, (HEADS, GROUP, lane), 2) // events
    )
    head_sum = (
        lax.broadcasted_iota(jnp.int32, (HEADS, HEADS * GROUP), 0)
        == lax.broadcasted_iota(jnp.int32, (HEADS, HEADS * GROUP), 1) // GROUP
    )
    head_sum = jnp.where(head_sum, 1.0, 0.0).astype(jnp.bfloat16)

    tiled_b = jnp.dot(
        both.astype(jnp.bfloat16), tile_ref[0], preferred_element_type=jnp.float32
    )
    block_of = lax.broadcasted_iota(jnp.int32, (lane, wide), 1) // STATE
    b_block = jnp.where(
        lax.broadcasted_iota(jnp.int32, (lane, wide), 0) // events == block_of,
        jnp.concatenate([tiled_b] * GROUP, axis=0),
        0.0,
    ).astype(jnp.bfloat16)
    r_rows = jnp.concatenate(
        [jnp.broadcast_to(reads[step], (GROUP, 128)) for step in range(STEPS)], axis=0
    )
    tiled_r = jnp.dot(r_rows.astype(jnp.bfloat16), tile_ref[1], preferred_element_type=jnp.float32)
    shape_r = (STEPS * GROUP, wide)
    r_block = jnp.where(
        lax.rem(lax.broadcasted_iota(jnp.int32, shape_r, 0), GROUP)
        == lax.broadcasted_iota(jnp.int32, shape_r, 1) // STATE,
        tiled_r,
        0.0,
    ).astype(jnp.bfloat16)
    diagonal = lax.broadcasted_iota(jnp.int32, (HEADS, 128), 0) == lax.broadcasted_iota(
        jnp.int32, (HEADS, 128), 1
    )
    decay = jnp.sum(jnp.where(diagonal, decay_both, 0.0), axis=1, keepdims=True)
    outs = STEPS * GROUP
    for q in range(spans):
        old = h_ref[0, :, q * wide : (q + 1) * wide]
        masked = jnp.where(own, flip_ref[:, q], 0.0).reshape(HEADS * GROUP, lane)
        x_rows = jnp.dot(
            head_sum, masked.astype(jnp.bfloat16), preferred_element_type=jnp.float32
        ).astype(jnp.bfloat16)
        update = jnp.dot(x_rows, b_block, preferred_element_type=jnp.float32)
        new_ref[0, :, q * wide : (q + 1) * wide] = (
            decay * old.astype(jnp.float32) + update
        ).astype(jnp.bfloat16)
        read_ref[:, q * outs : (q + 1) * outs] = lax.dot_general(
            old, r_block, (((1,), (1,)), ((), ())), preferred_element_type=jnp.float32
        )
    read = read_ref[...]
    on_head = (
        lax.broadcasted_iota(jnp.int32, (HEADS, inner), 0)
        == lax.broadcasted_iota(jnp.int32, (HEADS, inner), 1) // HEAD_DIM
    )
    results = []
    for step in range(STEPS):
        from_old = jnp.sum(
            jnp.where(on_head, split_dot(read, place_ref[step]), 0.0), axis=0, keepdims=True
        )
        mixed = jnp.sum(inputs * spread[events * (step + 1) : events * (step + 2)], axis=0, keepdims=True)
        at = events * (STEPS + 1) + step
        mixed = mixed + spread[at : at + 1] * from_old
        inv_rms = lax.rsqrt(jnp.mean(mixed * mixed, axis=1, keepdims=True) + 1e-05)
        results.append(mixed * inv_rms * gain_ref[...])
    out_ref[0] = jnp.concatenate(results, axis=0).astype(jnp.bfloat16)


def constants():
    inner = HEADS * HEAD_DIM

    def iota(shape, axis):
        return lax.broadcasted_iota(jnp.int32, shape, axis)

    big = (128, inner)
    expand = iota(big, 0) == iota(big, 1) // HEAD_DIM
    channel = iota(big, 1) % HEAD_DIM
    places = []
    for step in range(STEPS):
        lane = (channel // GROUP) * (STEPS * GROUP) + step * GROUP + channel % GROUP
        places.append(iota(big, 0) == lane)
    small = (128, GROUP * STATE)
    state_of = iota(small, 1) % STATE
    tiles = [iota(small, 0) == state_of, iota(small, 0) == state_of + STATE]
    return (
        expand.astype(jnp.bfloat16),
        jnp.stack(places).astype(jnp.bfloat16),
        jnp.stack(tiles).astype(jnp.bfloat16),
    )


def advance(proj, counts, state, window, params):
    conv_weight, conv_bias, dt_bias, decay_rate, skip_gain, norm_gain = params
    cached = state.shape[0]
    rows = proj.shape[0] // cached
    inner = HEADS * HEAD_DIM
    heads = jnp.pad(jnp.stack([dt_bias, decay_rate, skip_gain]), ((0, 5), (0, 128 - HEADS)))
    whole = [conv_weight, conv_bias[None], heads, norm_gain[None], *constants()]

    def same(array):
        return pl.BlockSpec(array.shape, lambda u, counts: (0,) * array.ndim)

    def own(array):
        return pl.BlockSpec((1,) + array.shape[1:], lambda u, counts: (u, 0, 0))

    result = jax.ShapeDtypeStruct((cached, STEPS, inner), jnp.bfloat16)
    return pl.pallas_call(
        user_kernel,
        grid_spec=pltpu.PrefetchScalarGridSpec(
            num_scalar_prefetch=1,
            grid=(cached,),
            in_specs=[
                pl.BlockSpec((rows, proj.shape[1]), lambda u, counts: (u, 0)),
                own(window),
                *[same(array) for array in whole],
                own(state),
            ],
            out_specs=[own(result), own(state), own(window)],
            scratch_shapes=[
                pltpu.VMEM((HEADS, HEAD_DIM // GROUP, GROUP, GROUP * rows), jnp.float32),
                pltpu.VMEM((HEADS, HEAD_DIM * STEPS), jnp.float32),
            ],
        ),
        out_shape=[
            result,
            jax.ShapeDtypeStruct(state.shape, jnp.bfloat16),
            jax.ShapeDtypeStruct(window.shape, jnp.bfloat16),
        ],
        compiler_params=pltpu.CompilerParams(vmem_limit_bytes=48 * 1024 * 1024),
    )(counts, proj, window, *whole, state)


MESH = pl.DeviceIdType.MESH


def project_kernel(
    sizes, tok_ref, w_ref, meta_ref, out_ref, meta_out,
    tokbuf, wbuf, acc, pbuf, sendbuf, recvbuf, metabuf,
    local_sem, tok_send, tok_recv, meta_send, meta_recv, plane_send, w_recv,
    up_send, down_send, row_send, row_recv,
):
    groups, owners, line, cached, users, length = sizes
    plane = groups * owners
    g = lax.axis_index("groups")
    r = lax.axis_index("req")
    f = lax.axis_index("fsdp")
    me = g * owners + r
    rows = tok_ref.shape[1]
    depth = w_ref.shape[0]
    wide = wbuf.shape[2]
    has_up = f < line - 1
    has_down = f > 0

    def at(q):
        return {"groups": q // owners, "req": lax.rem(q, owners), "fsdp": f}

    up = {"groups": g, "req": r, "fsdp": f + 1}
    down = {"groups": g, "req": r, "fsdp": f - 1}

    barrier = pltpu.get_barrier_semaphore()
    for p in range(1, plane):
        pl.semaphore_signal(
            barrier, inc=1, device_id=at(lax.rem(me + p, plane)), device_id_type=MESH
        )

    @pl.when(has_up)
    def _():
        pl.semaphore_signal(barrier, inc=1, device_id=up, device_id_type=MESH)

    @pl.when(has_down)
    def _():
        pl.semaphore_signal(barrier, inc=1, device_id=down, device_id_type=MESH)

    own_w = pltpu.make_async_copy(
        w_ref.at[:, pl.ds(pl.multiple_of(me * wide, 128), wide)],
        wbuf.at[f, pl.ds(pl.multiple_of(r * depth, depth), depth)],
        local_sem.at[0],
    )
    own_w.start()
    own_tok = pltpu.make_async_copy(tok_ref, tokbuf.at[me], local_sem.at[1])
    own_tok.start()
    own_meta = pltpu.make_async_copy(meta_ref, metabuf.at[me], local_sem.at[2])
    own_meta.start()
    pl.semaphore_wait(
        barrier, plane - 1 + has_up.astype(jnp.int32) + has_down.astype(jnp.int32)
    )

    def plane_copy(p):
        to = lax.rem(r + p, owners)
        q = g * owners + to
        return pltpu.make_async_remote_copy(
            src_ref=w_ref.at[:, pl.ds(pl.multiple_of(q * wide, 128), wide)],
            dst_ref=wbuf.at[f, pl.ds(pl.multiple_of(r * depth, depth), depth)],
            send_sem=plane_send.at[p],
            recv_sem=w_recv.at[f, r],
            device_id=at(q),
            device_id_type=MESH,
        )

    def line_copy(piece_f, piece_r, sems, target):
        block = wbuf.at[piece_f, pl.ds(pl.multiple_of(piece_r * depth, depth), depth)]
        return pltpu.make_async_remote_copy(
            src_ref=block,
            dst_ref=block,
            send_sem=sems.at[piece_f, piece_r],
            recv_sem=w_recv.at[piece_f, piece_r],
            device_id=target,
            device_id_type=MESH,
        )

    def peer_copy(src, dst, sends, recvs, p):
        return pltpu.make_async_remote_copy(
            src_ref=src,
            dst_ref=dst,
            send_sem=sends.at[p],
            recv_sem=recvs.at[p],
            device_id=at(lax.rem(me + p, plane)),
            device_id_type=MESH,
        )

    def tok_copy(p):
        return peer_copy(tok_ref, tokbuf.at[me], tok_send, tok_recv, p)

    def meta_copy(p):
        return peer_copy(meta_ref, metabuf.at[me], meta_send, meta_recv, p)

    def row_copy(p):
        q = lax.rem(me + p, plane)
        return peer_copy(sendbuf.at[q], recvbuf.at[me], row_send, row_recv, p)

    def send_up(piece_f, piece_r):
        @pl.when(has_up)
        def _():
            line_copy(piece_f, piece_r, up_send, up).start()

    def send_down(piece_f, piece_r):
        @pl.when(has_down)
        def _():
            line_copy(piece_f, piece_r, down_send, down).start()

    for p in range(1, owners):
        plane_copy(p).start()
    own_w.wait()
    send_up(f, r)
    send_down(f, r)
    for p in range(1, plane):
        meta_copy(p).start()
        tok_copy(p).start()
    for p in range(1, owners):
        came = lax.rem(r + owners - p, owners)
        line_copy(f, came, up_send, up).wait_recv()
        send_up(f, came)
        send_down(f, came)
    own_tok.wait()
    own_meta.wait()
    for p in range(1, plane):
        tok_copy(p).wait_recv()

    def partial_product(piece):
        return jnp.dot(
            tokbuf[:, piece].reshape(plane * rows, owners * depth),
            wbuf[piece],
            preferred_element_type=jnp.float32,
        )

    acc[...] = partial_product(f)
    for d in range(1, line):

        @pl.when(f - d >= 0)
        def _():
            for p in range(owners):
                piece_r = lax.rem(r + owners - p, owners)
                line_copy(f - d, piece_r, up_send, up).wait_recv()
                send_up(f - d, piece_r)

        @pl.when(f + d < line)
        def _():
            for p in range(owners):
                piece_r = lax.rem(r + owners - p, owners)
                line_copy(f + d, piece_r, down_send, down).wait_recv()
                send_down(f + d, piece_r)

        @pl.when(f - d >= 0)
        def _():
            acc[...] += partial_product(f - d)

        @pl.when(f + d < line)
        def _():
            acc[...] += partial_product(f + d)

    pbuf[...] = acc[...].astype(jnp.bfloat16).reshape(plane, rows, wide)
    for p in range(1, plane):
        meta_copy(p).wait_recv()

    items = cached * STEPS * length
    row = lax.broadcasted_iota(jnp.int32, (items, rows), 0)
    col = lax.broadcasted_iota(jnp.int32, (items, rows), 1)
    slot = row // (STEPS * length)
    same_event = lax.rem(row, STEPS * length) == (
        col // (users * length) * length + lax.rem(col, length)
    )

    def rows_for(p):
        q = lax.rem(me + p, plane)
        base = q // owners * owners
        wanted = lax.rem(q, owners) * cached + slot
        total = jnp.zeros((items, wide), jnp.float32)
        for source in range(owners):
            code = metabuf[base + source][0:1, 0:rows]
            pick = jnp.where((code == wanted) & same_event, 1.0, 0.0).astype(jnp.bfloat16)
            total = total + jnp.dot(
                pick, pbuf[base + source], preferred_element_type=jnp.float32
            )
        return total.astype(jnp.bfloat16)

    @pl.loop(1, plane)
    def _(p):
        sendbuf[lax.rem(me + p, plane)] = rows_for(p)
        row_copy(p).start()

    recvbuf[me] = rows_for(0)
    meta_out[...] = metabuf[...]
    for p in range(1, plane):
        row_copy(p).wait_recv()
    for q in range(plane):
        out_ref[:, q * wide : (q + 1) * wide] = recvbuf[q]
    for p in range(1, plane):
        tok_copy(p).wait_send()
        meta_copy(p).wait_send()
        row_copy(p).wait_send()
    for p in range(1, owners):
        plane_copy(p).wait_send()
    for d in range(line):

        @pl.when((f - d >= 0) & has_up)
        def _():
            for piece_r in range(owners):
                line_copy(f - d, piece_r, up_send, up).wait_send()

        @pl.when((f + d < line) & has_down)
        def _():
            for piece_r in range(owners):
                line_copy(f + d, piece_r, down_send, down).wait_send()


def project(tokens, weight, meta, sizes):
    groups, owners, line, cached, users, length = sizes
    plane = groups * owners
    rows = tokens.shape[1]
    depth = weight.shape[0]
    wide = weight.shape[1] // plane
    items = cached * STEPS * length
    dma = pltpu.SemaphoreType.DMA
    vmem = pl.BlockSpec(memory_space=pltpu.VMEM)
    return pl.pallas_call(
        functools.partial(project_kernel, sizes),
        in_specs=[vmem] * 3,
        out_specs=[vmem] * 2,
        out_shape=[
            jax.ShapeDtypeStruct((items, plane * wide), jnp.bfloat16),
            jax.ShapeDtypeStruct((plane,) + meta.shape, jnp.int32),
        ],
        scratch_shapes=[
            pltpu.VMEM((plane,) + tokens.shape, jnp.bfloat16),
            pltpu.VMEM((line, owners * depth, wide), jnp.bfloat16),
            pltpu.VMEM((plane * rows, wide), jnp.float32),
            pltpu.VMEM((plane, rows, wide), jnp.bfloat16),
            pltpu.VMEM((plane, items, wide), jnp.bfloat16),
            pltpu.VMEM((plane, items, wide), jnp.bfloat16),
            pltpu.VMEM((plane,) + meta.shape, jnp.int32),
            dma((3,)),
            dma((plane,)),
            dma((plane,)),
            dma((plane,)),
            dma((plane,)),
            dma((owners,)),
            dma((line, owners)),
            dma((line, owners)),
            dma((line, owners)),
            dma((plane,)),
            dma((plane,)),
        ],
        compiler_params=pltpu.CompilerParams(
            collective_id=0, has_side_effects=True, vmem_limit_bytes=56 * 1024 * 1024
        ),
    )(tokens, weight, meta)


def on_device(
    tokens,
    in_weight,
    dt_weight,
    conv_weight,
    conv_bias,
    dt_bias,
    decay_rate,
    skip_gain,
    norm_gain,
    state_cache,
    conv_cache,
    hash_owner,
    cache_slot,
    event_counts,
):
    owners = lax.axis_size("req")
    users = tokens.shape[1]
    length = tokens.shape[2]
    model = tokens.shape[3]
    cached = state_cache.shape[0]
    capacity = max(2, (2 * users + owners - 1) // owners)
    params = (conv_weight, conv_bias, dt_bias, decay_rate, skip_gain, norm_gain)
    groups = lax.axis_size("groups")
    line = lax.axis_size("fsdp")
    plane = groups * owners
    width = in_weight.shape[1]
    depth = in_weight.shape[0]
    wide = -(-(width + HEADS) // (128 * plane)) * 128
    both = jnp.concatenate(
        [
            in_weight,
            dt_weight,
            jnp.zeros((depth, plane * wide - width - HEADS), jnp.bfloat16),
        ],
        axis=1,
    )
    rows = STEPS * users * length
    tok = tokens.reshape(rows, owners, line, depth).transpose(2, 0, 1, 3)
    tok = tok.reshape(line, rows, owners * depth)

    def per_row(values):
        return jnp.repeat(values, length, axis=-1).reshape(-1)

    code = hash_owner * cached + cache_slot
    meta = jnp.stack(
        [per_row(jnp.stack([code] * STEPS)), per_row(event_counts)], axis=0
    ).astype(jnp.int32)
    meta = jnp.pad(meta, ((0, 6), (0, (-rows) % 128)), constant_values=-1)
    proj, all_meta = project(tok, both, meta, (groups, owners, line, cached, users, length))
    mine = lax.dynamic_slice_in_dim(all_meta, lax.axis_index("groups") * owners, owners, 0)
    mine = mine[:, :2, :rows].reshape(owners, 2, STEPS, users, length)[..., 0]
    codes = mine[:, 0, 0]
    came_counts = mine[:, 1]
    me = lax.axis_index("req")
    slots = jnp.arange(cached, dtype=jnp.int32)
    hit = codes[:, :, None] == me * cached + slots
    cache_counts = jnp.sum(
        hit[:, None].astype(jnp.int32) * came_counts[..., None], axis=(0, 2)
    ).T
    same = (codes[:, :, None] // cached == codes[:, None, :] // cached).astype(jnp.int32)
    before = jnp.tril(jnp.ones((users, users), jnp.int32), -1)
    ranks = jnp.sum(same * before, axis=2)
    turn = ranks[:, :, None] == jnp.arange(capacity, dtype=jnp.int32)
    route = jnp.sum(
        (turn[..., None] & hit[:, :, None, :]).astype(jnp.float32), axis=1
    ).astype(jnp.bfloat16)
    equal = (hash_owner[:, None] == hash_owner[None, :]).astype(jnp.int32)
    ranking = jnp.sum(equal * before, axis=1)
    stacked, new_states, work_window = advance(
        proj, cache_counts, state_cache, conv_cache, params
    )
    item_result = jnp.einsum(
        "ocs,sd->ocd",
        route,
        stacked.reshape(cached, -1),
        preferred_element_type=jnp.float32,
    )
    item_result = item_result.astype(jnp.bfloat16).reshape(owners, capacity, STEPS, -1)
    returned = lax.all_to_all(item_result, "req", split_axis=0, concat_axis=0, tiled=True)
    user_vectors = returned[hash_owner, ranking].transpose(1, 0, 2)
    return (user_vectors, new_states, work_window)


def solution(mesh):
    in_specs = (
        P(None, ("groups", "req", "fsdp"), None, None),
        P(("req", "fsdp"), None),
        P(("req", "fsdp"), None),
        P(),
        P(),
        P(),
        P(),
        P(),
        P(),
        P(("groups", "req", "fsdp"), None, None),
        P(("groups", "req", "fsdp"), None, None),
        P(("groups", "req", "fsdp")),
        P(("groups", "req", "fsdp")),
        P(None, ("groups", "req", "fsdp")),
    )
    out_specs = (
        P(None, ("groups", "req", "fsdp"), None),
        P(("groups", "req", "fsdp"), None, None),
        P(("groups", "req", "fsdp"), None, None),
    )
    return jax.shard_map(
        on_device, mesh=mesh, in_specs=in_specs, out_specs=out_specs, check_vma=False
    )
```

```python
import functools

import jax
import jax.numpy as jnp
from jax import lax
from jax.experimental import pallas as pl
from jax.experimental.pallas import tpu as pltpu
from jax.sharding import PartitionSpec as P

HEADS = 64
HEAD_DIM = 64
STATE = 64
STEPS = 2
GROUP = 8


def split_dot(value, picks):
    high = value.astype(jnp.bfloat16)
    low = (value - high.astype(jnp.float32)).astype(jnp.bfloat16)
    count = value.shape[0]
    parts = jnp.dot(
        jnp.concatenate([high, low], axis=0), picks, preferred_element_type=jnp.float32
    )
    return parts[0:count] + parts[count:]


def user_kernel(
    count_ref, proj_ref, window_ref, conv_ref, bias_ref, head_ref, gain_ref, expand_ref,
    place_ref, tile_ref, h_ref, out_ref, new_ref, window_out, flip_ref, read_ref,
):
    u = pl.program_id(0)
    taps = conv_ref.shape[0]
    width = conv_ref.shape[1]
    length = proj_ref.shape[0] // STEPS
    events = STEPS * length
    inner = HEADS * HEAD_DIM
    spans = HEAD_DIM // GROUP
    wide = GROUP * STATE
    lane = GROUP * events
    counts = [count_ref[u, step] for step in range(STEPS)]

    window = window_ref[0].astype(jnp.float32)
    ext_rows = lax.broadcasted_iota(jnp.int32, (length + taps - 1, width), 0)
    actives = []
    for step in range(STEPS):
        fresh = proj_ref[step * length : (step + 1) * length, 0:width].astype(jnp.float32)
        extended = jnp.concatenate([window, fresh], axis=0)
        conv_sum = bias_ref[...] + conv_ref[0:1] * extended[0:length]
        for tap in range(1, taps):
            conv_sum = conv_sum + conv_ref[tap : tap + 1] * extended[tap : tap + length]
        actives.append(conv_sum * jax.nn.sigmoid(conv_sum))
        window = jnp.concatenate(
            [
                jnp.sum(
                    jnp.where(ext_rows == counts[step] + w, extended, 0.0), axis=0, keepdims=True
                )
                for w in range(taps - 1)
            ],
            axis=0,
        )
    window_out[0] = window.astype(jnp.bfloat16)
    active = jnp.concatenate(actives, axis=0)
    inputs = active[:, 0:inner]
    both = active[:, inner:width]

    row = lax.broadcasted_iota(jnp.int32, (events, 128), 0)
    in_first = row < length
    limit = jnp.where(in_first, counts[0], length + counts[1])
    dt = proj_ref[:, width : width + 128].astype(jnp.float32) + head_ref[0:1]
    soft = jnp.maximum(dt, 0.0) + jnp.log1p(jnp.exp(-jnp.abs(dt)))
    step_size = jnp.where(row < limit, soft, 0.0)
    slope = -head_ref[1:2] * step_size
    one = slope[0:1]
    sums = [one]
    for t in range(1, events):
        one = slope[t : t + 1] + (0.0 if t == length else one)
        sums.append(one)
    cumulative = jnp.concatenate(sums, axis=0)
    total_0, total_1 = sums[length - 1], sums[events - 1]
    weight = jnp.exp(jnp.where(in_first, total_0, total_1) - cumulative) * step_size
    weight_end = jnp.where(in_first, jnp.exp(total_1), 1.0) * weight
    last = [
        (row == counts[0] - 1) & in_first,
        (row == length + counts[1] - 1) & (row >= length),
    ]
    reads = [jnp.sum(jnp.where(pick, both, 0.0), axis=0, keepdims=True) for pick in last]
    left = lax.broadcasted_iota(jnp.int32, (events, 128), 1) < STATE
    coefs = []
    for step in range(STEPS):
        turned = pltpu.roll(reads[step], STATE, 1)
        gram = jnp.sum(jnp.where(left, both * turned, 0.0), axis=1, keepdims=True)
        base = jnp.where(in_first, weight, 0.0) if step == 0 else weight_end
        coefs.append(base * gram + jnp.where(last[step], head_ref[2:3], 0.0))
    decay_0 = jnp.exp(total_0)
    decay_both = jnp.exp(total_0 + total_1)
    stacked = jnp.concatenate(
        [weight_end, coefs[0], coefs[1], decay_0, decay_both, jnp.zeros((14, 128), jnp.float32)],
        axis=0,
    )
    spread = split_dot(stacked, expand_ref[...])
    weighted = (inputs * spread[0:events]).astype(jnp.bfloat16)

    event_of = lax.rem(lax.broadcasted_iota(jnp.int32, (events, lane), 1), events)
    copies = (event_of == lax.broadcasted_iota(jnp.int32, (events, lane), 0)).astype(jnp.float32)
    flip_ref[...] = lax.dot_general(
        weighted,
        copies.astype(jnp.bfloat16),
        (((0,), (0,)), ((), ())),
        preferred_element_type=jnp.float32,
    ).reshape(HEADS, spans, GROUP, lane)
    own = (
        lax.broadcasted_iota(jnp.int32, (HEADS, GROUP, lane), 1)
        == lax.broadcasted_iota(jnp.int32, (HEADS, GROUP, lane), 2) // events
    )
    head_sum = (
        lax.broadcasted_iota(jnp.int32, (HEADS, HEADS * GROUP), 0)
        == lax.broadcasted_iota(jnp.int32, (HEADS, HEADS * GROUP), 1) // GROUP
    )
    head_sum = jnp.where(head_sum, 1.0, 0.0).astype(jnp.bfloat16)

    tiled_b = jnp.dot(
        both.astype(jnp.bfloat16), tile_ref[0], preferred_element_type=jnp.float32
    )
    block_of = lax.broadcasted_iota(jnp.int32, (lane, wide), 1) // STATE
    b_block = jnp.where(
        lax.broadcasted_iota(jnp.int32, (lane, wide), 0) // events == block_of,
        jnp.concatenate([tiled_b] * GROUP, axis=0),
        0.0,
    ).astype(jnp.bfloat16)
    r_rows = jnp.concatenate(
        [jnp.broadcast_to(reads[step], (GROUP, 128)) for step in range(STEPS)], axis=0
    )
    tiled_r = jnp.dot(r_rows.astype(jnp.bfloat16), tile_ref[1], preferred_element_type=jnp.float32)
    shape_r = (STEPS * GROUP, wide)
    r_block = jnp.where(
        lax.rem(lax.broadcasted_iota(jnp.int32, shape_r, 0), GROUP)
        == lax.broadcasted_iota(jnp.int32, shape_r, 1) // STATE,
        tiled_r,
        0.0,
    ).astype(jnp.bfloat16)
    diagonal = lax.broadcasted_iota(jnp.int32, (HEADS, 128), 0) == lax.broadcasted_iota(
        jnp.int32, (HEADS, 128), 1
    )
    decay = jnp.sum(jnp.where(diagonal, decay_both, 0.0), axis=1, keepdims=True)
    for q in range(spans):
        old = h_ref[0, :, q * wide : (q + 1) * wide]
        masked = jnp.where(own, flip_ref[:, q], 0.0).reshape(HEADS * GROUP, lane)
        x_rows = jnp.dot(
            head_sum, masked.astype(jnp.bfloat16), preferred_element_type=jnp.float32
        ).astype(jnp.bfloat16)
        update = jnp.dot(x_rows, b_block, preferred_element_type=jnp.float32)
        new_ref[0, :, q * wide : (q + 1) * wide] = (
            decay * old.astype(jnp.float32) + update
        ).astype(jnp.bfloat16)
        read = lax.dot_general(
            old, r_block, (((1,), (1,)), ((), ())), preferred_element_type=jnp.float32
        )
        for step in range(STEPS):
            read_ref[step * HEADS : (step + 1) * HEADS, q * GROUP : (q + 1) * GROUP] = read[
                :, step * GROUP : (step + 1) * GROUP
            ]
    placed = split_dot(read_ref[...], place_ref[...])
    on_head = (
        lax.broadcasted_iota(jnp.int32, (HEADS, inner), 0)
        == lax.broadcasted_iota(jnp.int32, (HEADS, inner), 1) // HEAD_DIM
    )
    results = []
    for step in range(STEPS):
        from_old = jnp.sum(
            jnp.where(on_head, placed[step * HEADS : (step + 1) * HEADS], 0.0),
            axis=0,
            keepdims=True,
        )
        mixed = jnp.sum(inputs * spread[events * (step + 1) : events * (step + 2)], axis=0, keepdims=True)
        at = events * (STEPS + 1) + step
        mixed = mixed + spread[at : at + 1] * from_old
        inv_rms = lax.rsqrt(jnp.mean(mixed * mixed, axis=1, keepdims=True) + 1e-05)
        results.append(mixed * inv_rms * gain_ref[...])
    out_ref[0] = jnp.concatenate(results, axis=0).astype(jnp.bfloat16)


def constants():
    inner = HEADS * HEAD_DIM

    def iota(shape, axis):
        return lax.broadcasted_iota(jnp.int32, shape, axis)

    big = (128, inner)
    expand = iota(big, 0) == iota(big, 1) // HEAD_DIM
    flat = (HEAD_DIM, inner)
    place = iota(flat, 0) == iota(flat, 1) % HEAD_DIM
    small = (128, GROUP * STATE)
    state_of = iota(small, 1) % STATE
    tiles = [iota(small, 0) == state_of, iota(small, 0) == state_of + STATE]
    return (
        expand.astype(jnp.bfloat16),
        place.astype(jnp.bfloat16),
        jnp.stack(tiles).astype(jnp.bfloat16),
    )


def advance(proj, counts, state, window, params):
    conv_weight, conv_bias, dt_bias, decay_rate, skip_gain, norm_gain = params
    cached = state.shape[0]
    rows = proj.shape[0] // cached
    inner = HEADS * HEAD_DIM
    heads = jnp.pad(jnp.stack([dt_bias, decay_rate, skip_gain]), ((0, 5), (0, 128 - HEADS)))
    whole = [conv_weight, conv_bias[None], heads, norm_gain[None], *constants()]

    def same(array):
        return pl.BlockSpec(array.shape, lambda u, counts: (0,) * array.ndim)

    def own(array):
        return pl.BlockSpec((1,) + array.shape[1:], lambda u, counts: (u, 0, 0))

    result = jax.ShapeDtypeStruct((cached, STEPS, inner), jnp.bfloat16)
    return pl.pallas_call(
        user_kernel,
        grid_spec=pltpu.PrefetchScalarGridSpec(
            num_scalar_prefetch=1,
            grid=(cached,),
            in_specs=[
                pl.BlockSpec((rows, proj.shape[1]), lambda u, counts: (u, 0)),
                own(window),
                *[same(array) for array in whole],
                own(state),
            ],
            out_specs=[own(result), own(state), own(window)],
            scratch_shapes=[
                pltpu.VMEM((HEADS, HEAD_DIM // GROUP, GROUP, GROUP * rows), jnp.float32),
                pltpu.VMEM((HEADS * STEPS, HEAD_DIM), jnp.float32),
            ],
        ),
        out_shape=[
            result,
            jax.ShapeDtypeStruct(state.shape, jnp.bfloat16),
            jax.ShapeDtypeStruct(window.shape, jnp.bfloat16),
        ],
        compiler_params=pltpu.CompilerParams(vmem_limit_bytes=48 * 1024 * 1024),
    )(counts, proj, window, *whole, state)


MESH = pl.DeviceIdType.MESH


def project_kernel(
    sizes, tok_ref, w_ref, meta_ref, out_ref, meta_out,
    tokbuf, wbuf, acc, pbuf, sendbuf, recvbuf, metabuf,
    local_sem, tok_send, tok_recv, meta_send, meta_recv, plane_send, w_recv,
    up_send, down_send, row_send, row_recv,
):
    groups, owners, line, cached, users, length = sizes
    plane = groups * owners
    g = lax.axis_index("groups")
    r = lax.axis_index("req")
    f = lax.axis_index("fsdp")
    me = g * owners + r
    rows = tok_ref.shape[1]
    depth = w_ref.shape[0]
    wide = wbuf.shape[2]
    has_up = f < line - 1
    has_down = f > 0

    def at(q):
        return {"groups": q // owners, "req": lax.rem(q, owners), "fsdp": f}

    up = {"groups": g, "req": r, "fsdp": f + 1}
    down = {"groups": g, "req": r, "fsdp": f - 1}

    barrier = pltpu.get_barrier_semaphore()
    for p in range(1, plane):
        pl.semaphore_signal(
            barrier, inc=1, device_id=at(lax.rem(me + p, plane)), device_id_type=MESH
        )

    @pl.when(has_up)
    def _():
        pl.semaphore_signal(barrier, inc=1, device_id=up, device_id_type=MESH)

    @pl.when(has_down)
    def _():
        pl.semaphore_signal(barrier, inc=1, device_id=down, device_id_type=MESH)

    own_w = pltpu.make_async_copy(
        w_ref.at[:, pl.ds(pl.multiple_of(me * wide, 128), wide)],
        wbuf.at[f, pl.ds(pl.multiple_of(r * depth, depth), depth)],
        local_sem.at[0],
    )
    own_w.start()
    own_tok = pltpu.make_async_copy(tok_ref, tokbuf.at[me], local_sem.at[1])
    own_tok.start()
    own_meta = pltpu.make_async_copy(meta_ref, metabuf.at[me], local_sem.at[2])
    own_meta.start()
    pl.semaphore_wait(
        barrier, plane - 1 + has_up.astype(jnp.int32) + has_down.astype(jnp.int32)
    )

    def plane_copy(p):
        to = lax.rem(r + p, owners)
        q = g * owners + to
        return pltpu.make_async_remote_copy(
            src_ref=w_ref.at[:, pl.ds(pl.multiple_of(q * wide, 128), wide)],
            dst_ref=wbuf.at[f, pl.ds(pl.multiple_of(r * depth, depth), depth)],
            send_sem=plane_send.at[p],
            recv_sem=w_recv.at[f, r],
            device_id=at(q),
            device_id_type=MESH,
        )

    def line_copy(piece_f, piece_r, sems, target):
        block = wbuf.at[piece_f, pl.ds(pl.multiple_of(piece_r * depth, depth), depth)]
        return pltpu.make_async_remote_copy(
            src_ref=block,
            dst_ref=block,
            send_sem=sems.at[piece_f, piece_r],
            recv_sem=w_recv.at[piece_f, piece_r],
            device_id=target,
            device_id_type=MESH,
        )

    def peer_copy(src, dst, sends, recvs, p):
        return pltpu.make_async_remote_copy(
            src_ref=src,
            dst_ref=dst,
            send_sem=sends.at[p],
            recv_sem=recvs.at[p],
            device_id=at(lax.rem(me + p, plane)),
            device_id_type=MESH,
        )

    def tok_copy(p):
        return peer_copy(tok_ref, tokbuf.at[me], tok_send, tok_recv, p)

    def meta_copy(p):
        return peer_copy(meta_ref, metabuf.at[me], meta_send, meta_recv, p)

    def row_copy(p):
        q = lax.rem(me + p, plane)
        return peer_copy(sendbuf.at[q], recvbuf.at[me], row_send, row_recv, p)

    def send_up(piece_f, piece_r):
        @pl.when(has_up)
        def _():
            line_copy(piece_f, piece_r, up_send, up).start()

    def send_down(piece_f, piece_r):
        @pl.when(has_down)
        def _():
            line_copy(piece_f, piece_r, down_send, down).start()

    for p in range(1, owners):
        plane_copy(p).start()
    own_w.wait()
    send_up(f, r)
    send_down(f, r)
    for p in range(1, plane):
        meta_copy(p).start()
        tok_copy(p).start()
    for p in range(1, owners):
        came = lax.rem(r + owners - p, owners)
        line_copy(f, came, up_send, up).wait_recv()
        send_up(f, came)
        send_down(f, came)
    own_tok.wait()
    own_meta.wait()
    for p in range(1, plane):
        tok_copy(p).wait_recv()

    def partial_product(piece):
        return jnp.dot(
            tokbuf[:, piece].reshape(plane * rows, owners * depth),
            wbuf[piece],
            preferred_element_type=jnp.float32,
        )

    acc[...] = partial_product(f)
    for d in range(1, line):

        @pl.when(f - d >= 0)
        def _():
            for p in range(owners):
                piece_r = lax.rem(r + owners - p, owners)
                line_copy(f - d, piece_r, up_send, up).wait_recv()
                send_up(f - d, piece_r)

        @pl.when(f + d < line)
        def _():
            for p in range(owners):
                piece_r = lax.rem(r + owners - p, owners)
                line_copy(f + d, piece_r, down_send, down).wait_recv()
                send_down(f + d, piece_r)

        @pl.when(f - d >= 0)
        def _():
            acc[...] += partial_product(f - d)

        @pl.when(f + d < line)
        def _():
            acc[...] += partial_product(f + d)

    pbuf[...] = acc[...].astype(jnp.bfloat16).reshape(plane, rows, wide)
    for p in range(1, plane):
        meta_copy(p).wait_recv()

    items = cached * STEPS * length
    row = lax.broadcasted_iota(jnp.int32, (items, rows), 0)
    col = lax.broadcasted_iota(jnp.int32, (items, rows), 1)
    slot = row // (STEPS * length)
    same_event = lax.rem(row, STEPS * length) == (
        col // (users * length) * length + lax.rem(col, length)
    )

    def rows_for(p):
        q = lax.rem(me + p, plane)
        base = q // owners * owners
        wanted = lax.rem(q, owners) * cached + slot
        total = jnp.zeros((items, wide), jnp.float32)
        for source in range(owners):
            code = metabuf[base + source][0:1, 0:rows]
            pick = jnp.where((code == wanted) & same_event, 1.0, 0.0).astype(jnp.bfloat16)
            total = total + jnp.dot(
                pick, pbuf[base + source], preferred_element_type=jnp.float32
            )
        return total.astype(jnp.bfloat16)

    @pl.loop(1, plane)
    def _(p):
        sendbuf[lax.rem(me + p, plane)] = rows_for(p)
        row_copy(p).start()

    recvbuf[me] = rows_for(0)
    meta_out[...] = metabuf[...]
    for p in range(1, plane):
        row_copy(p).wait_recv()
    for q in range(plane):
        out_ref[:, q * wide : (q + 1) * wide] = recvbuf[q]
    for p in range(1, plane):
        tok_copy(p).wait_send()
        meta_copy(p).wait_send()
        row_copy(p).wait_send()
    for p in range(1, owners):
        plane_copy(p).wait_send()
    for d in range(line):

        @pl.when((f - d >= 0) & has_up)
        def _():
            for piece_r in range(owners):
                line_copy(f - d, piece_r, up_send, up).wait_send()

        @pl.when((f + d < line) & has_down)
        def _():
            for piece_r in range(owners):
                line_copy(f + d, piece_r, down_send, down).wait_send()


def project(tokens, weight, meta, sizes):
    groups, owners, line, cached, users, length = sizes
    plane = groups * owners
    rows = tokens.shape[1]
    depth = weight.shape[0]
    wide = weight.shape[1] // plane
    items = cached * STEPS * length
    dma = pltpu.SemaphoreType.DMA
    vmem = pl.BlockSpec(memory_space=pltpu.VMEM)
    return pl.pallas_call(
        functools.partial(project_kernel, sizes),
        in_specs=[vmem] * 3,
        out_specs=[vmem] * 2,
        out_shape=[
            jax.ShapeDtypeStruct((items, plane * wide), jnp.bfloat16),
            jax.ShapeDtypeStruct((plane,) + meta.shape, jnp.int32),
        ],
        scratch_shapes=[
            pltpu.VMEM((plane,) + tokens.shape, jnp.bfloat16),
            pltpu.VMEM((line, owners * depth, wide), jnp.bfloat16),
            pltpu.VMEM((plane * rows, wide), jnp.float32),
            pltpu.VMEM((plane, rows, wide), jnp.bfloat16),
            pltpu.VMEM((plane, items, wide), jnp.bfloat16),
            pltpu.VMEM((plane, items, wide), jnp.bfloat16),
            pltpu.VMEM((plane,) + meta.shape, jnp.int32),
            dma((3,)),
            dma((plane,)),
            dma((plane,)),
            dma((plane,)),
            dma((plane,)),
            dma((owners,)),
            dma((line, owners)),
            dma((line, owners)),
            dma((line, owners)),
            dma((plane,)),
            dma((plane,)),
        ],
        compiler_params=pltpu.CompilerParams(
            collective_id=0, has_side_effects=True, vmem_limit_bytes=56 * 1024 * 1024
        ),
    )(tokens, weight, meta)


def on_device(
    tokens,
    in_weight,
    dt_weight,
    conv_weight,
    conv_bias,
    dt_bias,
    decay_rate,
    skip_gain,
    norm_gain,
    state_cache,
    conv_cache,
    hash_owner,
    cache_slot,
    event_counts,
):
    owners = lax.axis_size("req")
    users = tokens.shape[1]
    length = tokens.shape[2]
    model = tokens.shape[3]
    cached = state_cache.shape[0]
    capacity = max(2, (2 * users + owners - 1) // owners)
    params = (conv_weight, conv_bias, dt_bias, decay_rate, skip_gain, norm_gain)
    groups = lax.axis_size("groups")
    line = lax.axis_size("fsdp")
    plane = groups * owners
    width = in_weight.shape[1]
    depth = in_weight.shape[0]
    wide = -(-(width + HEADS) // (128 * plane)) * 128
    both = jnp.concatenate(
        [
            in_weight,
            dt_weight,
            jnp.zeros((depth, plane * wide - width - HEADS), jnp.bfloat16),
        ],
        axis=1,
    )
    rows = STEPS * users * length
    tok = tokens.reshape(rows, owners, line, depth).transpose(2, 0, 1, 3)
    tok = tok.reshape(line, rows, owners * depth)

    def per_row(values):
        return jnp.repeat(values, length, axis=-1).reshape(-1)

    code = hash_owner * cached + cache_slot
    meta = jnp.stack(
        [per_row(jnp.stack([code] * STEPS)), per_row(event_counts)], axis=0
    ).astype(jnp.int32)
    meta = jnp.pad(meta, ((0, 6), (0, (-rows) % 128)), constant_values=-1)
    proj, all_meta = project(tok, both, meta, (groups, owners, line, cached, users, length))
    mine = lax.dynamic_slice_in_dim(all_meta, lax.axis_index("groups") * owners, owners, 0)
    mine = mine[:, :2, :rows].reshape(owners, 2, STEPS, users, length)[..., 0]
    codes = mine[:, 0, 0]
    came_counts = mine[:, 1]
    me = lax.axis_index("req")
    slots = jnp.arange(cached, dtype=jnp.int32)
    hit = codes[:, :, None] == me * cached + slots
    cache_counts = jnp.sum(
        hit[:, None].astype(jnp.int32) * came_counts[..., None], axis=(0, 2)
    ).T
    same = (codes[:, :, None] // cached == codes[:, None, :] // cached).astype(jnp.int32)
    before = jnp.tril(jnp.ones((users, users), jnp.int32), -1)
    ranks = jnp.sum(same * before, axis=2)
    turn = ranks[:, :, None] == jnp.arange(capacity, dtype=jnp.int32)
    route = jnp.sum(
        (turn[..., None] & hit[:, :, None, :]).astype(jnp.float32), axis=1
    ).astype(jnp.bfloat16)
    equal = (hash_owner[:, None] == hash_owner[None, :]).astype(jnp.int32)
    ranking = jnp.sum(equal * before, axis=1)
    stacked, new_states, work_window = advance(
        proj, cache_counts, state_cache, conv_cache, params
    )
    item_result = jnp.einsum(
        "ocs,sd->ocd",
        route,
        stacked.reshape(cached, -1),
        preferred_element_type=jnp.float32,
    )
    item_result = item_result.astype(jnp.bfloat16).reshape(owners, capacity, STEPS, -1)
    returned = lax.all_to_all(item_result, "req", split_axis=0, concat_axis=0, tiled=True)
    user_vectors = returned[hash_owner, ranking].transpose(1, 0, 2)
    return (user_vectors, new_states, work_window)


def solution(mesh):
    in_specs = (
        P(None, ("groups", "req", "fsdp"), None, None),
        P(("req", "fsdp"), None),
        P(("req", "fsdp"), None),
        P(),
        P(),
        P(),
        P(),
        P(),
        P(),
        P(("groups", "req", "fsdp"), None, None),
        P(("groups", "req", "fsdp"), None, None),
        P(("groups", "req", "fsdp")),
        P(("groups", "req", "fsdp")),
        P(None, ("groups", "req", "fsdp")),
    )
    out_specs = (
        P(None, ("groups", "req", "fsdp"), None),
        P(("groups", "req", "fsdp"), None, None),
        P(("groups", "req", "fsdp"), None, None),
    )
    return jax.shard_map(
        on_device, mesh=mesh, in_specs=in_specs, out_specs=out_specs, check_vma=False
    )
```

```python
import functools

import jax
import jax.numpy as jnp
from jax import lax
from jax.experimental import pallas as pl
from jax.experimental.pallas import tpu as pltpu
from jax.sharding import PartitionSpec as P

HEADS = 64
HEAD_DIM = 64
STATE = 64
STEPS = 2
GROUP = 8


def split_dot(value, picks):
    high = value.astype(jnp.bfloat16)
    low = (value - high.astype(jnp.float32)).astype(jnp.bfloat16)
    count = value.shape[0]
    parts = jnp.dot(
        jnp.concatenate([high, low], axis=0), picks, preferred_element_type=jnp.float32
    )
    return parts[0:count] + parts[count:]


def user_kernel(
    count_ref, proj_ref, window_ref, conv_ref, bias_ref, head_ref, gain_ref, expand_ref,
    place_ref, tile_ref, h_ref, out_ref, new_ref, window_out, flip_ref, read_ref,
):
    u = pl.program_id(0)
    taps = conv_ref.shape[0]
    width = conv_ref.shape[1]
    length = proj_ref.shape[0] // STEPS
    events = STEPS * length
    inner = HEADS * HEAD_DIM
    spans = HEAD_DIM // GROUP
    wide = GROUP * STATE
    lane = GROUP * events
    counts = [count_ref[u, step] for step in range(STEPS)]

    window = window_ref[0].astype(jnp.float32)
    ext_rows = lax.broadcasted_iota(jnp.int32, (length + taps - 1, width), 0)
    actives = []
    for step in range(STEPS):
        fresh = proj_ref[step * length : (step + 1) * length, 0:width].astype(jnp.float32)
        extended = jnp.concatenate([window, fresh], axis=0)
        conv_sum = bias_ref[...] + conv_ref[0:1] * extended[0:length]
        for tap in range(1, taps):
            conv_sum = conv_sum + conv_ref[tap : tap + 1] * extended[tap : tap + length]
        actives.append(conv_sum * jax.nn.sigmoid(conv_sum))
        window = jnp.concatenate(
            [
                jnp.sum(
                    jnp.where(ext_rows == counts[step] + w, extended, 0.0), axis=0, keepdims=True
                )
                for w in range(taps - 1)
            ],
            axis=0,
        )
    window_out[0] = window.astype(jnp.bfloat16)
    active = jnp.concatenate(actives, axis=0)
    inputs = active[:, 0:inner]
    both = active[:, inner:width]

    row = lax.broadcasted_iota(jnp.int32, (events, 128), 0)
    in_first = row < length
    limit = jnp.where(in_first, counts[0], length + counts[1])
    dt = proj_ref[:, width : width + 128].astype(jnp.float32) + head_ref[0:1]
    soft = jnp.maximum(dt, 0.0) + jnp.log1p(jnp.exp(-jnp.abs(dt)))
    step_size = jnp.where(row < limit, soft, 0.0)
    slope = -head_ref[1:2] * step_size
    one = slope[0:1]
    sums = [one]
    for t in range(1, events):
        one = slope[t : t + 1] + (0.0 if t == length else one)
        sums.append(one)
    cumulative = jnp.concatenate(sums, axis=0)
    total_0, total_1 = sums[length - 1], sums[events - 1]
    weight = jnp.exp(jnp.where(in_first, total_0, total_1) - cumulative) * step_size
    weight_end = jnp.where(in_first, jnp.exp(total_1), 1.0) * weight
    last = [
        (row == counts[0] - 1) & in_first,
        (row == length + counts[1] - 1) & (row >= length),
    ]
    reads = [jnp.sum(jnp.where(pick, both, 0.0), axis=0, keepdims=True) for pick in last]
    left = lax.broadcasted_iota(jnp.int32, (events, 128), 1) < STATE
    coefs = []
    for step in range(STEPS):
        turned = pltpu.roll(reads[step], STATE, 1)
        gram = jnp.sum(jnp.where(left, both * turned, 0.0), axis=1, keepdims=True)
        base = jnp.where(in_first, weight, 0.0) if step == 0 else weight_end
        coefs.append(base * gram + jnp.where(last[step], head_ref[2:3], 0.0))
    decay_0 = jnp.exp(total_0)
    decay_both = jnp.exp(total_0 + total_1)
    stacked = jnp.concatenate(
        [weight_end, coefs[0], coefs[1], decay_0, decay_both, jnp.zeros((14, 128), jnp.float32)],
        axis=0,
    )
    spread = split_dot(stacked, expand_ref[...])
    weighted = (inputs * spread[0:events]).astype(jnp.bfloat16)

    event_of = lax.rem(lax.broadcasted_iota(jnp.int32, (events, lane), 1), events)
    copies = (event_of == lax.broadcasted_iota(jnp.int32, (events, lane), 0)).astype(jnp.float32)
    flip_ref[...] = lax.dot_general(
        weighted,
        copies.astype(jnp.bfloat16),
        (((0,), (0,)), ((), ())),
        preferred_element_type=jnp.float32,
    ).reshape(HEADS, spans, GROUP, lane)
    own = (
        lax.broadcasted_iota(jnp.int32, (HEADS, GROUP, lane), 1)
        == lax.broadcasted_iota(jnp.int32, (HEADS, GROUP, lane), 2) // events
    )
    head_sum = (
        lax.broadcasted_iota(jnp.int32, (HEADS, HEADS * GROUP), 0)
        == lax.broadcasted_iota(jnp.int32, (HEADS, HEADS * GROUP), 1) // GROUP
    )
    head_sum = jnp.where(head_sum, 1.0, 0.0).astype(jnp.bfloat16)

    tiled_b = jnp.dot(
        both.astype(jnp.bfloat16), tile_ref[0], preferred_element_type=jnp.float32
    )
    block_of = lax.broadcasted_iota(jnp.int32, (lane, wide), 1) // STATE
    b_block = jnp.where(
        lax.broadcasted_iota(jnp.int32, (lane, wide), 0) // events == block_of,
        jnp.concatenate([tiled_b] * GROUP, axis=0),
        0.0,
    ).astype(jnp.bfloat16)
    r_rows = jnp.concatenate(
        [jnp.broadcast_to(reads[step], (GROUP, 128)) for step in range(STEPS)], axis=0
    )
    tiled_r = jnp.dot(r_rows.astype(jnp.bfloat16), tile_ref[1], preferred_element_type=jnp.float32)
    shape_r = (STEPS * GROUP, wide)
    r_block = jnp.where(
        lax.rem(lax.broadcasted_iota(jnp.int32, shape_r, 0), GROUP)
        == lax.broadcasted_iota(jnp.int32, shape_r, 1) // STATE,
        tiled_r,
        0.0,
    ).astype(jnp.bfloat16)
    diagonal = lax.broadcasted_iota(jnp.int32, (HEADS, 128), 0) == lax.broadcasted_iota(
        jnp.int32, (HEADS, 128), 1
    )
    decay = jnp.sum(jnp.where(diagonal, decay_both, 0.0), axis=1, keepdims=True)
    for q in range(spans):
        old = h_ref[0, :, q * wide : (q + 1) * wide]
        masked = jnp.where(own, flip_ref[:, q], 0.0).reshape(HEADS * GROUP, lane)
        x_rows = jnp.dot(
            head_sum, masked.astype(jnp.bfloat16), preferred_element_type=jnp.float32
        ).astype(jnp.bfloat16)
        update = jnp.dot(x_rows, b_block, preferred_element_type=jnp.float32)
        new_ref[0, :, q * wide : (q + 1) * wide] = (
            decay * old.astype(jnp.float32) + update
        ).astype(jnp.bfloat16)
        read = lax.dot_general(
            old, r_block, (((1,), (1,)), ((), ())), preferred_element_type=jnp.float32
        )
        for step in range(STEPS):
            read_ref[step * HEADS : (step + 1) * HEADS, q * GROUP : (q + 1) * GROUP] = read[
                :, step * GROUP : (step + 1) * GROUP
            ]
    placed = split_dot(read_ref[...], place_ref[...])
    on_head = (
        lax.broadcasted_iota(jnp.int32, (HEADS, inner), 0)
        == lax.broadcasted_iota(jnp.int32, (HEADS, inner), 1) // HEAD_DIM
    )
    results = []
    for step in range(STEPS):
        from_old = jnp.sum(
            jnp.where(on_head, placed[step * HEADS : (step + 1) * HEADS], 0.0),
            axis=0,
            keepdims=True,
        )
        mixed = jnp.sum(inputs * spread[events * (step + 1) : events * (step + 2)], axis=0, keepdims=True)
        at = events * (STEPS + 1) + step
        mixed = mixed + spread[at : at + 1] * from_old
        inv_rms = lax.rsqrt(jnp.mean(mixed * mixed, axis=1, keepdims=True) + 1e-05)
        results.append(mixed * inv_rms * gain_ref[...])
    out_ref[0] = jnp.concatenate(results, axis=0).astype(jnp.bfloat16)


def constants():
    inner = HEADS * HEAD_DIM

    def iota(shape, axis):
        return lax.broadcasted_iota(jnp.int32, shape, axis)

    big = (128, inner)
    expand = iota(big, 0) == iota(big, 1) // HEAD_DIM
    flat = (HEAD_DIM, inner)
    place = iota(flat, 0) == iota(flat, 1) % HEAD_DIM
    small = (128, GROUP * STATE)
    state_of = iota(small, 1) % STATE
    tiles = [iota(small, 0) == state_of, iota(small, 0) == state_of + STATE]
    return (
        expand.astype(jnp.bfloat16),
        place.astype(jnp.bfloat16),
        jnp.stack(tiles).astype(jnp.bfloat16),
    )


def advance(proj, counts, state, window, params):
    conv_weight, conv_bias, dt_bias, decay_rate, skip_gain, norm_gain = params
    cached = state.shape[0]
    rows = proj.shape[0] // cached
    inner = HEADS * HEAD_DIM
    heads = jnp.pad(jnp.stack([dt_bias, decay_rate, skip_gain]), ((0, 5), (0, 128 - HEADS)))
    whole = [conv_weight, conv_bias[None], heads, norm_gain[None], *constants()]

    def same(array):
        return pl.BlockSpec(array.shape, lambda u, counts: (0,) * array.ndim)

    def own(array):
        return pl.BlockSpec((1,) + array.shape[1:], lambda u, counts: (u, 0, 0))

    result = jax.ShapeDtypeStruct((cached, STEPS, inner), jnp.bfloat16)
    return pl.pallas_call(
        user_kernel,
        grid_spec=pltpu.PrefetchScalarGridSpec(
            num_scalar_prefetch=1,
            grid=(cached,),
            in_specs=[
                pl.BlockSpec((rows, proj.shape[1]), lambda u, counts: (u, 0)),
                own(window),
                *[same(array) for array in whole],
                own(state),
            ],
            out_specs=[own(result), own(state), own(window)],
            scratch_shapes=[
                pltpu.VMEM((HEADS, HEAD_DIM // GROUP, GROUP, GROUP * rows), jnp.float32),
                pltpu.VMEM((HEADS * STEPS, HEAD_DIM), jnp.float32),
            ],
        ),
        out_shape=[
            result,
            jax.ShapeDtypeStruct(state.shape, jnp.bfloat16),
            jax.ShapeDtypeStruct(window.shape, jnp.bfloat16),
        ],
        compiler_params=pltpu.CompilerParams(vmem_limit_bytes=48 * 1024 * 1024),
    )(counts, proj, window, *whole, state)


MESH = pl.DeviceIdType.MESH


def project_kernel(
    sizes, tok_ref, w_ref, meta_ref, out_ref, meta_out,
    tokbuf, wbuf, acc, pbuf, sendbuf, recvbuf, metabuf,
    local_sem, tok_send, tok_recv, meta_send, meta_recv, plane_send, w_recv,
    up_send, down_send, row_send, row_recv,
):
    groups, owners, line, cached, users, length, narrow = sizes
    plane = groups * owners
    g = lax.axis_index("groups")
    r = lax.axis_index("req")
    f = lax.axis_index("fsdp")
    me = g * owners + r
    rows = tok_ref.shape[1]
    depth = w_ref.shape[0]
    wide = wbuf.shape[2]
    odd = lax.rem(me, 2) == 1
    has_up = f < line - 1
    has_down = f > 0

    def start_of(q):
        return q // 2 * (wide + narrow) + lax.rem(q, 2) * wide

    def at(q):
        return {"groups": q // owners, "req": lax.rem(q, owners), "fsdp": f}

    up = {"groups": g, "req": r, "fsdp": f + 1}
    down = {"groups": g, "req": r, "fsdp": f - 1}

    wbuf[:, :, narrow:] = jnp.zeros((line, owners * depth, wide - narrow), jnp.bfloat16)
    barrier = pltpu.get_barrier_semaphore()
    for p in range(1, plane):
        pl.semaphore_signal(
            barrier, inc=1, device_id=at(lax.rem(me + p, plane)), device_id_type=MESH
        )

    @pl.when(has_up)
    def _():
        pl.semaphore_signal(barrier, inc=1, device_id=up, device_id_type=MESH)

    @pl.when(has_down)
    def _():
        pl.semaphore_signal(barrier, inc=1, device_id=down, device_id_type=MESH)

    own_w = pltpu.make_async_copy(
        w_ref.at[:, pl.ds(pl.multiple_of(start_of(me), 128), wide)],
        wbuf.at[f, pl.ds(pl.multiple_of(r * depth, depth), depth)],
        local_sem.at[0],
    )
    own_w.start()
    own_tok = pltpu.make_async_copy(tok_ref, tokbuf.at[me], local_sem.at[1])
    own_tok.start()
    own_meta = pltpu.make_async_copy(meta_ref, metabuf.at[me], local_sem.at[2])
    own_meta.start()
    pl.semaphore_wait(
        barrier, plane - 1 + has_up.astype(jnp.int32) + has_down.astype(jnp.int32)
    )

    def plane_copy(p):
        to = lax.rem(r + p, owners)
        q = g * owners + to
        return pltpu.make_async_remote_copy(
            src_ref=w_ref.at[:, pl.ds(pl.multiple_of(start_of(q), 128), wide)],
            dst_ref=wbuf.at[f, pl.ds(pl.multiple_of(r * depth, depth), depth)],
            send_sem=plane_send.at[p],
            recv_sem=w_recv.at[f, r],
            device_id=at(q),
            device_id_type=MESH,
        )

    def line_copy(piece_f, piece_r, sems, target, columns=wide):
        block = wbuf.at[
            piece_f, pl.ds(pl.multiple_of(piece_r * depth, depth), depth), pl.ds(0, columns)
        ]
        return pltpu.make_async_remote_copy(
            src_ref=block,
            dst_ref=block,
            send_sem=sems.at[piece_f, piece_r],
            recv_sem=w_recv.at[piece_f, piece_r],
            device_id=target,
            device_id_type=MESH,
        )

    def peer_copy(src, dst, sends, recvs, p):
        return pltpu.make_async_remote_copy(
            src_ref=src,
            dst_ref=dst,
            send_sem=sends.at[p],
            recv_sem=recvs.at[p],
            device_id=at(lax.rem(me + p, plane)),
            device_id_type=MESH,
        )

    def tok_copy(p):
        return peer_copy(tok_ref, tokbuf.at[me], tok_send, tok_recv, p)

    def meta_copy(p):
        return peer_copy(meta_ref, metabuf.at[me], meta_send, meta_recv, p)

    def row_copy(p):
        q = lax.rem(me + p, plane)
        return peer_copy(sendbuf.at[q], recvbuf.at[me], row_send, row_recv, p)

    def send_up(piece_f, piece_r):
        @pl.when(has_up & odd)
        def _():
            line_copy(piece_f, piece_r, up_send, up, narrow).start()

        @pl.when(has_up & jnp.logical_not(odd))
        def _():
            line_copy(piece_f, piece_r, up_send, up).start()

    def send_down(piece_f, piece_r):
        @pl.when(has_down & odd)
        def _():
            line_copy(piece_f, piece_r, down_send, down, narrow).start()

        @pl.when(has_down & jnp.logical_not(odd))
        def _():
            line_copy(piece_f, piece_r, down_send, down).start()

    def wait_line(piece_f, piece_r, sems, target):
        @pl.when(odd)
        def _():
            line_copy(piece_f, piece_r, sems, target, narrow).wait_recv()

        @pl.when(jnp.logical_not(odd))
        def _():
            line_copy(piece_f, piece_r, sems, target).wait_recv()

    def wait_sent(piece_f, piece_r, sems, target):
        @pl.when(odd)
        def _():
            line_copy(piece_f, piece_r, sems, target, narrow).wait_send()

        @pl.when(jnp.logical_not(odd))
        def _():
            line_copy(piece_f, piece_r, sems, target).wait_send()

    for p in range(1, owners):
        plane_copy(p).start()
    own_w.wait()
    send_up(f, r)
    send_down(f, r)
    for p in range(1, plane):
        meta_copy(p).start()
        tok_copy(p).start()
    for p in range(1, owners):
        came = lax.rem(r + owners - p, owners)
        line_copy(f, came, up_send, up).wait_recv()
        send_up(f, came)
        send_down(f, came)
    own_tok.wait()
    own_meta.wait()
    for p in range(1, plane):
        tok_copy(p).wait_recv()

    def partial_product(piece):
        return jnp.dot(
            tokbuf[:, piece].reshape(plane * rows, owners * depth),
            wbuf[piece],
            preferred_element_type=jnp.float32,
        )

    acc[...] = partial_product(f)
    for d in range(1, line):

        @pl.when(f - d >= 0)
        def _():
            for p in range(owners):
                piece_r = lax.rem(r + owners - p, owners)
                wait_line(f - d, piece_r, up_send, up)
                send_up(f - d, piece_r)

        @pl.when(f + d < line)
        def _():
            for p in range(owners):
                piece_r = lax.rem(r + owners - p, owners)
                wait_line(f + d, piece_r, down_send, down)
                send_down(f + d, piece_r)

        @pl.when(f - d >= 0)
        def _():
            acc[...] += partial_product(f - d)

        @pl.when(f + d < line)
        def _():
            acc[...] += partial_product(f + d)

    pbuf[...] = acc[...].astype(jnp.bfloat16).reshape(plane, rows, wide)
    for p in range(1, plane):
        meta_copy(p).wait_recv()

    items = cached * STEPS * length
    row = lax.broadcasted_iota(jnp.int32, (items, rows), 0)
    col = lax.broadcasted_iota(jnp.int32, (items, rows), 1)
    slot = row // (STEPS * length)
    same_event = lax.rem(row, STEPS * length) == (
        col // (users * length) * length + lax.rem(col, length)
    )

    def rows_for(p):
        q = lax.rem(me + p, plane)
        base = q // owners * owners
        wanted = lax.rem(q, owners) * cached + slot
        total = jnp.zeros((items, wide), jnp.float32)
        for source in range(owners):
            code = metabuf[base + source][0:1, 0:rows]
            pick = jnp.where((code == wanted) & same_event, 1.0, 0.0).astype(jnp.bfloat16)
            total = total + jnp.dot(
                pick, pbuf[base + source], preferred_element_type=jnp.float32
            )
        return total.astype(jnp.bfloat16)

    @pl.loop(1, plane)
    def _(p):
        sendbuf[lax.rem(me + p, plane)] = rows_for(p)
        row_copy(p).start()

    recvbuf[me] = rows_for(0)
    meta_out[...] = metabuf[...]
    for p in range(1, plane):
        row_copy(p).wait_recv()
    for q in range(plane):
        first = q // 2 * (wide + narrow) + q % 2 * wide
        out_ref[:, first : first + wide] = recvbuf[q]
    for p in range(1, plane):
        tok_copy(p).wait_send()
        meta_copy(p).wait_send()
        row_copy(p).wait_send()
    for p in range(1, owners):
        plane_copy(p).wait_send()
    for d in range(line):

        @pl.when((f - d >= 0) & has_up)
        def _():
            for piece_r in range(owners):
                wait_sent(f - d, piece_r, up_send, up)

        @pl.when((f + d < line) & has_down)
        def _():
            for piece_r in range(owners):
                wait_sent(f + d, piece_r, down_send, down)


def project(tokens, weight, meta, sizes):
    groups, owners, line, cached, users, length, narrow = sizes
    plane = groups * owners
    rows = tokens.shape[1]
    depth = weight.shape[0]
    pair = (weight.shape[1] - 128) // (plane // 2)
    wide = pair - narrow
    items = cached * STEPS * length
    dma = pltpu.SemaphoreType.DMA
    vmem = pl.BlockSpec(memory_space=pltpu.VMEM)
    return pl.pallas_call(
        functools.partial(project_kernel, sizes),
        in_specs=[vmem] * 3,
        out_specs=[vmem] * 2,
        out_shape=[
            jax.ShapeDtypeStruct((items, weight.shape[1]), jnp.bfloat16),
            jax.ShapeDtypeStruct((plane,) + meta.shape, jnp.int32),
        ],
        scratch_shapes=[
            pltpu.VMEM((plane,) + tokens.shape, jnp.bfloat16),
            pltpu.VMEM((line, owners * depth, wide), jnp.bfloat16),
            pltpu.VMEM((plane * rows, wide), jnp.float32),
            pltpu.VMEM((plane, rows, wide), jnp.bfloat16),
            pltpu.VMEM((plane, items, wide), jnp.bfloat16),
            pltpu.VMEM((plane, items, wide), jnp.bfloat16),
            pltpu.VMEM((plane,) + meta.shape, jnp.int32),
            dma((3,)),
            dma((plane,)),
            dma((plane,)),
            dma((plane,)),
            dma((plane,)),
            dma((owners,)),
            dma((line, owners)),
            dma((line, owners)),
            dma((line, owners)),
            dma((plane,)),
            dma((plane,)),
        ],
        compiler_params=pltpu.CompilerParams(
            collective_id=0, has_side_effects=True, vmem_limit_bytes=56 * 1024 * 1024
        ),
    )(tokens, weight, meta)


def on_device(
    tokens,
    in_weight,
    dt_weight,
    conv_weight,
    conv_bias,
    dt_bias,
    decay_rate,
    skip_gain,
    norm_gain,
    state_cache,
    conv_cache,
    hash_owner,
    cache_slot,
    event_counts,
):
    owners = lax.axis_size("req")
    users = tokens.shape[1]
    length = tokens.shape[2]
    model = tokens.shape[3]
    cached = state_cache.shape[0]
    capacity = max(2, (2 * users + owners - 1) // owners)
    params = (conv_weight, conv_bias, dt_bias, decay_rate, skip_gain, norm_gain)
    groups = lax.axis_size("groups")
    line = lax.axis_size("fsdp")
    plane = groups * owners
    width = in_weight.shape[1]
    depth = in_weight.shape[0]
    tiles = max(2, -(-(width + HEADS) // (64 * plane)))
    narrow = tiles // 2 * 128
    total = plane // 2 * tiles * 128 + 128
    both = jnp.concatenate(
        [
            in_weight,
            dt_weight,
            jnp.zeros((depth, total - width - HEADS), jnp.bfloat16),
        ],
        axis=1,
    )
    rows = STEPS * users * length
    tok = tokens.reshape(rows, owners, line, depth).transpose(2, 0, 1, 3)
    tok = tok.reshape(line, rows, owners * depth)

    def per_row(values):
        return jnp.repeat(values, length, axis=-1).reshape(-1)

    code = hash_owner * cached + cache_slot
    meta = jnp.stack(
        [per_row(jnp.stack([code] * STEPS)), per_row(event_counts)], axis=0
    ).astype(jnp.int32)
    meta = jnp.pad(meta, ((0, 6), (0, (-rows) % 128)), constant_values=-1)
    proj, all_meta = project(tok, both, meta, (groups, owners, line, cached, users, length, narrow))
    mine = lax.dynamic_slice_in_dim(all_meta, lax.axis_index("groups") * owners, owners, 0)
    mine = mine[:, :2, :rows].reshape(owners, 2, STEPS, users, length)[..., 0]
    codes = mine[:, 0, 0]
    came_counts = mine[:, 1]
    me = lax.axis_index("req")
    slots = jnp.arange(cached, dtype=jnp.int32)
    hit = codes[:, :, None] == me * cached + slots
    cache_counts = jnp.sum(
        hit[:, None].astype(jnp.int32) * came_counts[..., None], axis=(0, 2)
    ).T
    same = (codes[:, :, None] // cached == codes[:, None, :] // cached).astype(jnp.int32)
    before = jnp.tril(jnp.ones((users, users), jnp.int32), -1)
    ranks = jnp.sum(same * before, axis=2)
    turn = ranks[:, :, None] == jnp.arange(capacity, dtype=jnp.int32)
    route = jnp.sum(
        (turn[..., None] & hit[:, :, None, :]).astype(jnp.float32), axis=1
    ).astype(jnp.bfloat16)
    equal = (hash_owner[:, None] == hash_owner[None, :]).astype(jnp.int32)
    ranking = jnp.sum(equal * before, axis=1)
    stacked, new_states, work_window = advance(
        proj, cache_counts, state_cache, conv_cache, params
    )
    item_result = jnp.einsum(
        "ocs,sd->ocd",
        route,
        stacked.reshape(cached, -1),
        preferred_element_type=jnp.float32,
    )
    item_result = item_result.astype(jnp.bfloat16).reshape(owners, capacity, STEPS, -1)
    returned = lax.all_to_all(item_result, "req", split_axis=0, concat_axis=0, tiled=True)
    user_vectors = returned[hash_owner, ranking].transpose(1, 0, 2)
    return (user_vectors, new_states, work_window)


def solution(mesh):
    in_specs = (
        P(None, ("groups", "req", "fsdp"), None, None),
        P(("req", "fsdp"), None),
        P(("req", "fsdp"), None),
        P(),
        P(),
        P(),
        P(),
        P(),
        P(),
        P(("groups", "req", "fsdp"), None, None),
        P(("groups", "req", "fsdp"), None, None),
        P(("groups", "req", "fsdp")),
        P(("groups", "req", "fsdp")),
        P(None, ("groups", "req", "fsdp")),
    )
    out_specs = (
        P(None, ("groups", "req", "fsdp"), None),
        P(("groups", "req", "fsdp"), None, None),
        P(("groups", "req", "fsdp"), None, None),
    )
    return jax.shard_map(
        on_device, mesh=mesh, in_specs=in_specs, out_specs=out_specs, check_vma=False
    )
```
